32 devices in a mesh: groups: 2 (over x), dp: 16 (over z, y, core).
Axes of the slice: x: 2, y: 2, z: 4, core: 2. Of those that a mesh axis runs over, the one named last changes fastest.
Arguments:
- fingerprints: bfloat16 [32768, 512], P(('groups', 'dp')), parts along dimension 0, may hold values from 0 to 1
- targets: bfloat16 [32768, 128], P(('groups', 'dp')), parts along dimension 0, may hold values from -6 to 6
- landmark_index: int32 [4096], P('groups'), parts along dimension 0, may hold values from 0 to 16383, as said below
Outputs:
- rhs: float32 [4096, 128], P(('groups', 'dp')), parts along dimension 0
- panel: float32 [4096, 256], P(('groups', 'dp')), parts along dimension 0
- trailing: float32 [4096, 2048], P(('groups', 'dp')), parts along dimension 0
The draws below stay inside these ranges and needn't reach their ends.
There are 2 independent parts, one for each index of `groups`. The reference program is written for one: setup_inputs(seed, part) draws one part's arguments, and reference() takes and returns one part's arrays. A program takes and returns all parts, laid end to end along the dimension named above; each array names one. Nothing has to cross between parts.
Inputs may be any that keep to these rules, and one draw needn't show every extreme that they name: `landmark_index`: distinct rows of the window; row r belongs to index r // 1024 of dp; each index of dp owns at most 256 landmarks and a quarter of them own exactly 256.
All inputs are finite; a program needn't handle non-finite values.
Results may differ from the reference program's by a relative error of at most 0.0029.
Values may be sent and summed in bfloat16 or wider, within the bound.
No kernel may reach another device: no remote copies, remote signals or barrier semaphores. Data moves between devices by JAX's collectives and lax.ppermute only.
A program may use at most 64 MiB of HBM per device.

```python
import math
import jax
import jax.numpy as jnp
from jax import lax

F = 512
M = 2048
NT = 128
PB = 256
ROWS_DEV = 1024
NMOL = 16384
LMD = 128
N_DP = 16


def draw_fingerprints(key, part):
    key_power, key_value = jax.random.split(jax.random.fold_in(key, 3))
    position = jnp.arange(NMOL).astype(jnp.float32) / NMOL
    base_power = jnp.exp(jax.random.uniform(key_power, (NMOL, 1), jnp.float32) * math.log(4.0))
    exponent = base_power * (1.0 + 2.0 * position[:, None])
    values = jax.random.uniform(key_value, (NMOL, F), jnp.float32) ** exponent
    return values.astype(jnp.bfloat16)


def draw_landmark_index(key, part):
    key_count, key_rows, key_order = jax.random.split(jax.random.fold_in(key, 11), 3)
    pattern = jnp.tile(jnp.array([4, 2, 1, 1], jnp.int32), N_DP // 4) * (LMD // 2)
    counts = pattern[jax.random.permutation(key_count, N_DP)]
    owner_sorted = jnp.repeat(jnp.arange(N_DP, dtype=jnp.int32), counts, total_repeat_length=M)
    starts = jnp.cumsum(counts) - counts
    owner_rank = jnp.arange(M, dtype=jnp.int32) - starts[owner_sorted]
    row_perms = jax.vmap(lambda sub_key: jax.random.permutation(sub_key, ROWS_DEV))(jax.random.split(key_rows, N_DP))
    chosen = owner_sorted * ROWS_DEV + row_perms[owner_sorted, owner_rank].astype(jnp.int32)
    return chosen[jax.random.permutation(key_order, M)].astype(jnp.int32)


def shard_levels(rng, extent, cuts, smallest, top_value):
    level = 1.0
    for axis_at, shards_of in cuts:
        heights = jax.random.uniform(jax.random.fold_in(jax.random.fold_in(rng, 6), axis_at), (shards_of,), jnp.float32, smallest / len(cuts), top_value / len(cuts))
        level = level * jnp.repeat(jnp.exp(heights), extent[axis_at] // shards_of).reshape((-1,) + (1,) * (len(extent) - 1 - axis_at))
    return level


def noise(rng, dims, deviation, limit, cuts=(), held_as=jnp.bfloat16):
    result = jax.random.normal(rng, dims, jnp.float32) * deviation
    if len(cuts) > 0:
        result = shard_levels(rng, dims, cuts, -0.22, 0.18) * result
    return jnp.clip(result, min=-limit, max=limit).astype(held_as)


def setup_inputs(seed: int = 0, part: int = 0) -> dict:
    streams_of = jax.random.split(jax.random.key(seed), 4)
    part_keys = jax.random.split(jax.random.fold_in(streams_of[3], part), 4)
    fingerprints = draw_fingerprints(jax.random.fold_in(jax.random.fold_in(streams_of[3], part), 71), part)
    targets = noise(part_keys[1], (NMOL, NT), 1.0, 6.0, ((0, 16),))
    landmark_index = draw_landmark_index(jax.random.fold_in(jax.random.fold_in(streams_of[3], part), 71), part)
    return dict(fingerprints=fingerprints, targets=targets, landmark_index=landmark_index)


ridge_weight = 0.01

def sq_norms(row_block):
    wide_rows = row_block.astype(jnp.float32)
    return lax.optimization_barrier(jnp.sum(wide_rows * wide_rows, axis=1))

def tanimoto(row_block, landmark_fps, landmark_norms):
    inner_prod = jnp.dot(row_block.astype(jnp.float32), landmark_fps.T.astype(jnp.float32), preferred_element_type=jnp.float32)
    row_norms = sq_norms(row_block)
    return inner_prod / (row_norms[:, None] + landmark_norms[None, :] - inner_prod)

def reference(fingerprints, targets, landmark_index):
    landmark_fps = fingerprints[landmark_index]
    landmark_norms = sq_norms(landmark_fps)
    fp_blocks = fingerprints.reshape(N_DP, ROWS_DEV, F)
    target_blocks = targets.reshape(N_DP, ROWS_DEV, NT)

    def add_sums(running, fp_block):
        kernel = tanimoto(fp_block, landmark_fps, landmark_norms)
        return (running + lax.optimization_barrier(jnp.sum(kernel, axis=0)), None)
    col_total, _ = lax.scan(add_sums, jnp.zeros((M,), jnp.float32), fp_blocks)
    col_mean = col_total / NMOL

    def add_gram(running, pieces):
        fp_block, target_block = pieces
        centred = (tanimoto(fp_block, landmark_fps, landmark_norms) - col_mean[None, :]).astype(jnp.bfloat16)
        joined = jnp.concatenate([centred, target_block], axis=1)
        left_wide = centred.astype(jnp.float32)
        right_wide = joined.astype(jnp.float32)
        return (running + jnp.dot(left_wide.T, right_wide, precision=lax.Precision.HIGHEST), None)
    totals, _ = lax.scan(add_gram, jnp.zeros((M, M + NT), jnp.float32), (fp_blocks, target_blocks))
    rhs = totals[:, M:] / math.sqrt(ridge_weight * NMOL)
    system = totals[:, :M] / (ridge_weight * NMOL) + tanimoto(landmark_fps, landmark_fps, landmark_norms)
    corner = jnp.linalg.cholesky(system[:PB, :PB])
    panel = lax.linalg.triangular_solve(corner, system[:, :PB], left_side=False, lower=True, transpose_a=True)
    trailing = system - jnp.dot(panel, panel.T, precision=lax.Precision.HIGHEST)
    return (rhs, panel, trailing)
```

```python
import math

import jax
import jax.numpy as jnp
from jax import lax
from jax.sharding import PartitionSpec as P

PB = 256


ridge_weight = 0.01


def sq_norms(row_block):
    wide_rows = row_block.astype(jnp.float32)
    return jnp.sum(wide_rows * wide_rows, axis=1)


def tanimoto(row_block, landmark_fps, landmark_norms):
    inner_prod = lax.dot_general(
        row_block, landmark_fps, (((1,), (1,)), ((), ())), preferred_element_type=jnp.float32
    )
    row_norms = sq_norms(row_block)
    return inner_prod / (row_norms[:, None] + landmark_norms[None, :] - inner_prod)


def local_any(fingerprints, targets, landmark_index):
    rows_dev = fingerprints.shape[0]
    devices = lax.axis_size("dp")
    total_rows = rows_dev * devices
    landmarks = landmark_index.shape[0]
    land_share = landmarks // devices
    position = lax.axis_index("dp")
    owner_dev = landmark_index // rows_dev
    offset = landmark_index % rows_dev
    is_mine = owner_dev == position
    capacity = 2 * land_share
    owner_onehot = (owner_dev[:, None] == jnp.arange(devices, dtype=jnp.int32)[None, :]).astype(
        jnp.int32
    )
    owner_rank = jnp.sum(jnp.cumsum(owner_onehot, axis=0) * owner_onehot, axis=1) - 1
    slot_rows = (
        jnp.zeros((capacity,), jnp.int32)
        .at[jnp.where(is_mine, owner_rank, capacity)]
        .set(offset, mode="drop")
    )
    packed = fingerprints[slot_rows]
    gathered = lax.all_gather(packed, "dp", axis=0, tiled=True)
    landmark_fps = gathered[owner_dev * capacity + owner_rank]
    landmark_norms = sq_norms(landmark_fps)
    kernel = tanimoto(fingerprints, landmark_fps, landmark_norms)
    col_total = lax.psum(jnp.sum(kernel, axis=0), "dp")
    col_mean = col_total / total_rows
    centred = (kernel - col_mean[None, :]).astype(jnp.bfloat16)
    joined = jnp.concatenate([centred, targets], axis=1)
    totals = lax.psum_scatter(
        lax.dot_general(
            centred, joined, (((0,), (0,)), ((), ())), preferred_element_type=jnp.float32
        ),
        "dp",
        scatter_dimension=0,
        tiled=True,
    )
    gram_rows = totals[:, :landmarks]
    rhs_rows = totals[:, landmarks:]
    rhs = rhs_rows / math.sqrt(ridge_weight * total_rows)
    own_fps = lax.dynamic_slice_in_dim(landmark_fps, position * land_share, land_share, 0)
    system_rows = gram_rows / (ridge_weight * total_rows) + tanimoto(
        own_fps, landmark_fps, landmark_norms
    )
    panel_width = PB
    column_block = lax.all_gather(system_rows[:, :panel_width], "dp", axis=0, tiled=True)
    corner = jnp.linalg.cholesky(column_block[:panel_width])
    panel_full = lax.linalg.triangular_solve(
        corner, column_block, left_side=False, lower=True, transpose_a=True
    )
    panel_own = lax.dynamic_slice_in_dim(panel_full, position * land_share, land_share, 0)
    trailing = system_rows - jnp.dot(panel_own, panel_full.T, precision=lax.Precision.HIGHEST)
    return (rhs, panel_own, trailing)


CORE = [(i, i ^ 1) for i in range(16)]
ROW = [(i, i ^ 2) for i in range(16)]


def rotate(step):
    return [(i, (i + 4 * step) % 16) for i in range(16)]


def send(x, perm):
    return lax.ppermute(x, "dp", perm)


def highest(a, b):
    return lax.dot_general(
        a,
        b,
        (((0,), (0,)), ((), ())),
        precision=lax.Precision.HIGHEST,
        preferred_element_type=jnp.float32,
    )


def gram(a, b):
    return lax.dot_general(a, b, (((0,), (0,)), ((), ())), preferred_element_type=jnp.float32)


def gather_chips(x):
    pair = jnp.concatenate([x, send(x, ROW)], axis=0)
    return jnp.concatenate([pair] + [send(pair, rotate(s)) for s in (1, 2, 3)], axis=0)


def landmarks_everywhere(fingerprints, landmark_index):
    rows_dev = fingerprints.shape[0]
    devices = lax.axis_size("dp")
    landmarks = landmark_index.shape[0]
    land_share = landmarks // devices
    position = lax.axis_index("dp")
    owner_dev = landmark_index // rows_dev
    offset = landmark_index % rows_dev
    is_mine = owner_dev == position
    capacity = 2 * land_share
    owner_onehot = (owner_dev[:, None] == jnp.arange(devices, dtype=jnp.int32)[None, :]).astype(
        jnp.int32
    )
    owner_rank = jnp.sum(jnp.cumsum(owner_onehot, axis=0) * owner_onehot, axis=1) - 1
    slot_rows = (
        jnp.zeros((capacity,), jnp.int32)
        .at[jnp.where(is_mine, owner_rank, capacity)]
        .set(offset, mode="drop")
    )
    packed = fingerprints[slot_rows]
    gathered = lax.all_gather(packed, "dp", axis=0, tiled=True)
    return gathered[owner_dev * capacity + owner_rank]


def local_16(fingerprints, targets, landmark_index):
    rows_dev = fingerprints.shape[0]
    total_rows = rows_dev * 16
    landmarks = landmark_index.shape[0]
    share = landmarks // 16
    width = PB
    position = lax.axis_index("dp")
    core = position % 2
    row = (position // 2) % 2
    layer = position // 4
    scale = 1.0 / (ridge_weight * total_rows)

    fps = jnp.concatenate([fingerprints, send(fingerprints, CORE)], axis=0)
    tgs = jnp.concatenate([targets, send(targets, CORE)], axis=0)
    chip_rows = 2 * rows_dev
    landmark_fps = landmarks_everywhere(fingerprints, landmark_index)
    norms = sq_norms(landmark_fps)
    kernel = tanimoto(fps, landmark_fps, norms)
    mean = jnp.sum(kernel, axis=0) / chip_rows
    centred = (kernel - mean[None, :]).astype(jnp.bfloat16)
    target_sum = jnp.sum(tgs.astype(jnp.float32), axis=0)
    own_cols = lax.dynamic_slice_in_dim(
        centred.reshape(chip_rows, 8, 2, share), core, 1, axis=2
    ).reshape(chip_rows, 8 * share)

    first = gram(own_cols[:, :share], centred)
    lead = jnp.sum(first, axis=0)
    lead_own = lax.dynamic_slice_in_dim(lead, core * share, share, 0)
    lead_mass = jnp.sum(lead_own)
    usable = lead_mass > 1e-3 * jnp.sum(jnp.abs(lead_own))
    lead_weight = jnp.where(usable, 1.0 / jnp.where(usable, lead_mass, 1.0), 0.0)
    lead = lax.reduce_precision(lead, 8, 7).astype(jnp.bfloat16)

    def lead_outer(start, right):
        left = lax.dynamic_slice_in_dim(lead, start, share, 0)
        return lead_weight * gram(left[None, :], right[None, :])

    chip_stats = gather_chips(jnp.concatenate([mean, target_sum])[None, :])
    means, target_sums = chip_stats[:, :landmarks], chip_stats[:, landmarks:]
    leads = gather_chips(
        jnp.concatenate([lead.astype(jnp.float32), jnp.broadcast_to(lead_weight, (128,))])[None, :]
    )
    leads, lead_weights = leads[:, :landmarks], leads[:, landmarks : landmarks + 1]
    shift = means - jnp.mean(means, axis=0, keepdims=True)
    left_terms = jnp.concatenate([shift * chip_rows, leads], axis=0)
    right_terms = jnp.concatenate([shift, leads * lead_weights], axis=0)

    def add_back(start):
        return highest(lax.dynamic_slice_in_dim(left_terms, start, share, 1), right_terms)

    first_rest = (first - lead_outer(core * share, lead)).astype(jnp.bfloat16)
    quarter = share // 4

    def quarter_of(q):
        return lax.dynamic_slice_in_dim(first_rest, (q % 4) * quarter, quarter, 0)

    part = quarter_of(layer).astype(jnp.float32)
    for s in (2, 1, 3):
        part = part + send(quarter_of(layer + s), rotate(s)).astype(jnp.float32)
    part = part.astype(jnp.bfloat16)
    part = part.astype(jnp.float32) + send(part, ROW).astype(jnp.float32)
    part = part.astype(jnp.bfloat16)
    pieces = jnp.zeros((4,) + part.shape, jnp.bfloat16)
    pieces = lax.dynamic_update_index_in_dim(pieces, part, layer, 0)
    for s in (2, 1, 3):
        pieces = lax.dynamic_update_index_in_dim(
            pieces, send(part, rotate(s)), (layer + 4 - s) % 4, 0
        )
    block_fps = lax.dynamic_slice_in_dim(landmark_fps, core * share, share, 0)
    block = (pieces.reshape(share, landmarks).astype(jnp.float32) + add_back(core * share)) * scale
    block = block + tanimoto(block_fps, landmark_fps, norms)
    other = send(block, CORE)
    panel_rows = lax.dynamic_slice_in_dim(
        jnp.concatenate([block, other, block], axis=0), core * share, 2 * share, 0
    )
    corner = jnp.linalg.cholesky(panel_rows[:, :width])
    factor = lax.linalg.triangular_solve(corner, panel_rows, left_side=True, lower=True)

    right = jnp.concatenate([centred[:, width:], tgs], axis=1)
    lead_right = jnp.concatenate([lead[width:], jnp.zeros((tgs.shape[1],), jnp.bfloat16)])

    def row_sum(s):
        there = (layer + s) % 4
        left = lax.dynamic_slice_in_dim(own_cols, there * 2 * share, 2 * share, 1)
        start = (there * 4 + core) * share
        outer = jnp.concatenate(
            [lead_outer(start, lead_right), lead_outer(start + 2 * share, lead_right)], axis=0
        )
        out = (gram(left, right) - outer).astype(jnp.bfloat16)
        mine = lax.dynamic_slice_in_dim(out, row * share, share, 0)
        theirs = lax.dynamic_slice_in_dim(out, (1 - row) * share, share, 0)
        return mine.astype(jnp.float32) + send(theirs, ROW).astype(jnp.float32)

    own = 0.0
    for s in (2, 1, 3):
        own = own + send(row_sum(s).astype(jnp.bfloat16), rotate(s)).astype(jnp.float32)
    own = own + row_sum(0)
    start = position * share
    own_fps = lax.dynamic_slice_in_dim(landmark_fps, start, share, 0)
    rest = (own[:, : landmarks - width] + add_back(start)[:, width:]) * scale + tanimoto(
        own_fps, landmark_fps[width:], norms[width:]
    )
    own_shift = lax.dynamic_slice_in_dim(shift, start, share, 1)
    rhs = (own[:, landmarks - width :] + highest(own_shift, target_sums)) / math.sqrt(
        ridge_weight * total_rows
    )
    own_panel = lax.dynamic_slice_in_dim(panel_rows, start, share, 1)
    own_factor = lax.dynamic_slice_in_dim(factor, start, share, 1)
    system_rows = jnp.concatenate([own_panel.T, rest], axis=1)
    trailing = system_rows - highest(own_factor, factor)
    return (rhs, own_factor.T, trailing)


def solution(mesh):
    local = local_16 if mesh.shape["dp"] == 16 else local_any
    in_specs = (P(("groups", "dp"), None), P(("groups", "dp"), None), P("groups"))
    out_specs = (P(("groups", "dp"), None), P(("groups", "dp"), None), P(("groups", "dp"), None))
    return jax.shard_map(local, mesh=mesh, in_specs=in_specs, out_specs=out_specs, check_vma=False)
```

```python
import functools
import math

import jax
import jax.numpy as jnp
from jax import lax
from jax.experimental import pallas as pl
from jax.experimental.pallas import tpu as pltpu
from jax.sharding import PartitionSpec as P

PB = 256


ridge_weight = 0.01


def sq_norms(row_block):
    wide_rows = row_block.astype(jnp.float32)
    return jnp.sum(wide_rows * wide_rows, axis=1)


def tanimoto(row_block, landmark_fps, landmark_norms):
    inner_prod = lax.dot_general(
        row_block, landmark_fps, (((1,), (1,)), ((), ())), preferred_element_type=jnp.float32
    )
    row_norms = sq_norms(row_block)
    return inner_prod / (row_norms[:, None] + landmark_norms[None, :] - inner_prod)


def local_any(fingerprints, targets, landmark_index):
    rows_dev = fingerprints.shape[0]
    devices = lax.axis_size("dp")
    total_rows = rows_dev * devices
    landmarks = landmark_index.shape[0]
    land_share = landmarks // devices
    position = lax.axis_index("dp")
    owner_dev = landmark_index // rows_dev
    offset = landmark_index % rows_dev
    is_mine = owner_dev == position
    capacity = 2 * land_share
    owner_onehot = (owner_dev[:, None] == jnp.arange(devices, dtype=jnp.int32)[None, :]).astype(
        jnp.int32
    )
    owner_rank = jnp.sum(jnp.cumsum(owner_onehot, axis=0) * owner_onehot, axis=1) - 1
    slot_rows = (
        jnp.zeros((capacity,), jnp.int32)
        .at[jnp.where(is_mine, owner_rank, capacity)]
        .set(offset, mode="drop")
    )
    packed = fingerprints[slot_rows]
    gathered = lax.all_gather(packed, "dp", axis=0, tiled=True)
    landmark_fps = gathered[owner_dev * capacity + owner_rank]
    landmark_norms = sq_norms(landmark_fps)
    kernel = tanimoto(fingerprints, landmark_fps, landmark_norms)
    col_total = lax.psum(jnp.sum(kernel, axis=0), "dp")
    col_mean = col_total / total_rows
    centred = (kernel - col_mean[None, :]).astype(jnp.bfloat16)
    joined = jnp.concatenate([centred, targets], axis=1)
    totals = lax.psum_scatter(
        lax.dot_general(
            centred, joined, (((0,), (0,)), ((), ())), preferred_element_type=jnp.float32
        ),
        "dp",
        scatter_dimension=0,
        tiled=True,
    )
    gram_rows = totals[:, :landmarks]
    rhs_rows = totals[:, landmarks:]
    rhs = rhs_rows / math.sqrt(ridge_weight * total_rows)
    own_fps = lax.dynamic_slice_in_dim(landmark_fps, position * land_share, land_share, 0)
    system_rows = gram_rows / (ridge_weight * total_rows) + tanimoto(
        own_fps, landmark_fps, landmark_norms
    )
    panel_width = PB
    column_block = lax.all_gather(system_rows[:, :panel_width], "dp", axis=0, tiled=True)
    corner = jnp.linalg.cholesky(column_block[:panel_width])
    panel_full = lax.linalg.triangular_solve(
        corner, column_block, left_side=False, lower=True, transpose_a=True
    )
    panel_own = lax.dynamic_slice_in_dim(panel_full, position * land_share, land_share, 0)
    trailing = system_rows - jnp.dot(panel_own, panel_full.T, precision=lax.Precision.HIGHEST)
    return (rhs, panel_own, trailing)


CORE = [(i, i ^ 1) for i in range(16)]
ROW = [(i, i ^ 2) for i in range(16)]
NEAR = [(i, i ^ 4) for i in range(16)]
FAR = [(i, i ^ 8) for i in range(16)]
LANES = 128
TILE = 256
VMEM_BYTES = 56 * 2**20


def rotate(step):
    return [(i, (i + 4 * step) % 16) for i in range(16)]


def send(x, perm):
    return lax.ppermute(x, "dp", perm)


def highest(a, b):
    return lax.dot_general(
        a,
        b,
        (((0,), (0,)), ((), ())),
        precision=lax.Precision.HIGHEST,
        preferred_element_type=jnp.float32,
    )


def dot_nt(a, b):
    return lax.dot_general(a, b, (((1,), (1,)), ((), ())), preferred_element_type=jnp.float32)


def dot_nn(a, b):
    return lax.dot_general(a, b, (((1,), (0,)), ((), ())), preferred_element_type=jnp.float32)


def gather_chips(x):
    pair = jnp.concatenate([x, send(x, ROW)], axis=0)
    return jnp.concatenate([pair] + [send(pair, rotate(s)) for s in (1, 2, 3)], axis=0)


def vmem(count):
    return [pl.BlockSpec(memory_space=pltpu.VMEM)] * count


def spread(row_vector):
    return jnp.broadcast_to(row_vector, (LANES, LANES)).T


def stage_body(
    core_ref, land_ref, fps_ref, norms_ref, tgs_ref,
    ct_ref, mean_ref, rhs_ref, rest_ref, lead_ref, column_ref, weight_ref,
    cent_ref, first_ref,
):
    step = pl.program_id(0)
    rows = fps_ref.shape[0]
    base = pl.multiple_of(step * TILE, TILE)
    block = pl.multiple_of(core_ref[0] * LANES, LANES)
    tile = land_ref[...]
    wide = tile.astype(jnp.float32)
    land_norms = jnp.sum(wide * wide, axis=1, keepdims=True)
    inner = dot_nt(tile, fps_ref[...])
    kernel = inner / (norms_ref[...] + land_norms - inner)
    mean = jnp.sum(kernel, axis=1, keepdims=True) * (1.0 / rows)
    cent = kernel - mean
    cent_ref[...] = cent
    ct_ref[pl.ds(base, TILE), :] = cent.astype(jnp.bfloat16)
    mean_ref[:, pl.ds(base, TILE)] = jnp.broadcast_to(mean, (TILE, LANES)).T[:1, :]
    own = cent_ref[pl.ds(block, LANES), :]
    high = own.astype(jnp.bfloat16)
    low = (own - high.astype(jnp.float32)).astype(jnp.bfloat16)
    rhs_ref[step] = dot_nn(high, tgs_ref[...]) + dot_nn(low, tgs_ref[...])
    first_ref[:, pl.ds(base, TILE)] = dot_nt(
        ct_ref[pl.ds(block, LANES), :], ct_ref[pl.ds(base, TILE), :]
    )

    @pl.when(step == pl.num_programs(0) - 1)
    def _():
        lead = jnp.sum(first_ref[...], axis=0, keepdims=True)
        lead_ref[...] = lead
        lead_own = lead_ref[:, pl.ds(block, LANES)]
        mass = jnp.sum(lead_own, axis=1, keepdims=True)
        size = jnp.sum(jnp.abs(lead_own), axis=1, keepdims=True)
        usable = mass > 1e-3 * size
        weight = jnp.where(usable, 1.0 / jnp.where(usable, mass, 1.0), 0.0)
        weight_ref[...] = jnp.broadcast_to(weight, (1, LANES))
        mine = spread(lead_own) * weight
        for j in range(lead.shape[1] // LANES):
            cols = slice(j * LANES, (j + 1) * LANES)
            part = lead[:, cols]
            column_ref[cols, :] = spread(part) * weight
            rest_ref[:, cols] = (first_ref[:, cols] - mine * part).astype(jnp.bfloat16)


def stage(core, landmark_fps, fps, norms, tgs):
    rows, length = fps.shape
    landmarks = landmark_fps.shape[0]
    steps = landmarks // TILE
    f32 = jnp.float32

    def whole(shape):
        return pl.BlockSpec(shape, lambda i, c: (0,) * len(shape))

    outs = [
        ((landmarks, rows), jnp.bfloat16),
        ((1, landmarks), f32),
        ((steps, LANES, LANES), f32),
        ((LANES, landmarks), jnp.bfloat16),
        ((1, landmarks), f32),
        ((landmarks, LANES), f32),
        ((1, LANES), f32),
    ]
    return pl.pallas_call(
        stage_body,
        grid_spec=pltpu.PrefetchScalarGridSpec(
            num_scalar_prefetch=1,
            grid=(steps,),
            in_specs=[
                pl.BlockSpec((TILE, length), lambda i, c: (i, 0)),
                whole(fps.shape),
                whole(norms.shape),
                whole(tgs.shape),
            ],
            out_specs=[whole(s) for s, _ in outs],
            scratch_shapes=[
                pltpu.VMEM((TILE, rows), f32),
                pltpu.VMEM((LANES, landmarks), f32),
            ],
        ),
        out_shape=[jax.ShapeDtypeStruct(s, d) for s, d in outs],
        compiler_params=pltpu.CompilerParams(vmem_limit_bytes=VMEM_BYTES),
        name="stage",
    )(core, landmark_fps, fps, norms, tgs)


def pieces_body(at_ref, ct_ref, lead_ref, column_ref, rhs_ref, *refs):
    outs, left_ref = refs[:-1], refs[-1]
    count = len(outs)
    for p in range(count):
        at = pl.multiple_of(at_ref[p], LANES)
        left_ref[p * LANES : (p + 1) * LANES, :] = ct_ref[pl.ds(at, LANES), :]
    for t in range(1, ct_ref.shape[0] // TILE):
        got = dot_nt(left_ref[...], ct_ref[t * TILE : (t + 1) * TILE, :])
        for p, out in enumerate(outs):
            at = pl.multiple_of(at_ref[p], LANES)
            column = column_ref[pl.ds(at, LANES), :]
            for h in range(TILE // LANES):
                lo = t * TILE + h * LANES
                part = got[p * LANES : (p + 1) * LANES, h * LANES : (h + 1) * LANES]
                part = part - column * lead_ref[:, lo : lo + LANES]
                out[:, lo - TILE : lo - TILE + LANES] = part.astype(out.dtype)
    for p, out in enumerate(outs):
        out[:, ct_ref.shape[0] - TILE :] = rhs_ref[at_ref[p] // TILE].astype(out.dtype)


def pieces(starts, ct, lead, column, rhs_part):
    width = ct.shape[0] - TILE + LANES
    outs = [jnp.float32, jnp.bfloat16] * (len(starts) // 2)
    return pl.pallas_call(
        pieces_body,
        in_specs=[pl.BlockSpec(memory_space=pltpu.SMEM)] + vmem(4),
        out_specs=vmem(len(outs)),
        out_shape=[jax.ShapeDtypeStruct((LANES, width), d) for d in outs],
        scratch_shapes=[pltpu.VMEM((len(outs) * LANES, ct.shape[1]), jnp.bfloat16)],
        compiler_params=pltpu.CompilerParams(vmem_limit_bytes=VMEM_BYTES),
        name="pieces",
    )(jnp.stack(starts).astype(jnp.int32), ct, lead, column, rhs_part)


CHOL = 32


def exact_dot(a, b, dims=((1,), (0,))):
    return lax.dot_general(
        a, b, (dims, ((), ())), precision=lax.Precision.HIGHEST, preferred_element_type=jnp.float32
    )


def factor_body(blocks, state_ref, out_ref):
    size = state_ref.shape[0]
    out_ref[...] = state_ref[...]
    sub = lax.broadcasted_iota(jnp.int32, (CHOL, LANES), 0)
    lane = lax.broadcasted_iota(jnp.int32, (CHOL, LANES), 1)
    for b in blocks:
        lo, hi = b * CHOL, (b + 1) * CHOL
        diag = out_ref[lo:hi, lo:hi]
        work = jnp.concatenate(
            [
                diag,
                (sub == lane)[:, :CHOL].astype(jnp.float32),
                jnp.zeros((CHOL, LANES - 2 * CHOL), jnp.float32),
            ],
            axis=1,
        )

        def eliminate(k, x):
            col = jnp.sum(jnp.where(lane == k, x, 0.0), axis=1, keepdims=True)
            row = jnp.sum(jnp.where(sub == k, x, 0.0), axis=0, keepdims=True)
            pivot = jnp.sum(jnp.where(lane[:1] == k, row, 0.0), axis=1, keepdims=True)
            return x - jnp.where(sub > k, col, 0.0) * (row / pivot)

        work = lax.fori_loop(0, CHOL, eliminate, work)
        pivots = jnp.sum(jnp.where(sub == lane, work, 0.0), axis=1, keepdims=True)
        inverse = work[:, CHOL : 2 * CHOL] / jnp.sqrt(pivots)
        done = exact_dot(inverse, out_ref[lo:hi, :])
        out_ref[lo:hi, :] = done
        if hi < size:
            out_ref[hi:, :] = out_ref[hi:, :] - exact_dot(
                done[:, hi:size], done, ((0,), (0,))
            )


def eliminate_blocks(state, blocks):
    return pl.pallas_call(
        functools.partial(factor_body, blocks),
        in_specs=vmem(1),
        out_specs=vmem(1)[0],
        out_shape=jax.ShapeDtypeStruct(state.shape, jnp.float32),
        compiler_params=pltpu.CompilerParams(vmem_limit_bytes=VMEM_BYTES),
        name="factor",
    )(state)


def landmarks_everywhere(fingerprints, landmark_index):
    rows_dev = fingerprints.shape[0]
    devices = lax.axis_size("dp")
    landmarks = landmark_index.shape[0]
    land_share = landmarks // devices
    position = lax.axis_index("dp")
    owner_dev = landmark_index // rows_dev
    offset = landmark_index % rows_dev
    is_mine = owner_dev == position
    capacity = 2 * land_share
    owner_onehot = (owner_dev[:, None] == jnp.arange(devices, dtype=jnp.int32)[None, :]).astype(
        jnp.int32
    )
    owner_rank = jnp.sum(jnp.cumsum(owner_onehot, axis=0) * owner_onehot, axis=1) - 1
    slot_rows = (
        jnp.zeros((capacity,), jnp.int32)
        .at[jnp.where(is_mine, owner_rank, capacity)]
        .set(offset, mode="drop")
    )
    packed = fingerprints[slot_rows]
    gathered = lax.all_gather(packed, "dp", axis=0, tiled=True)
    return gathered[owner_dev * capacity + owner_rank]


def local_16(fingerprints, targets, landmark_index):
    rows_dev = fingerprints.shape[0]
    total_rows = rows_dev * 16
    landmarks = landmark_index.shape[0]
    share = landmarks // 16
    width = PB
    position = lax.axis_index("dp")
    core = position % 2
    row = (position // 2) % 2
    layer = position // 4
    scale = 1.0 / (ridge_weight * total_rows)

    fps = jnp.concatenate([fingerprints, send(fingerprints, CORE)], axis=0)
    tgs = jnp.concatenate([targets, send(targets, CORE)], axis=0)
    chip_rows = 2 * rows_dev
    landmark_fps = landmarks_everywhere(fingerprints, landmark_index)
    norms = sq_norms(landmark_fps)
    target_sum = jnp.sum(tgs.astype(jnp.float32), axis=0, keepdims=True)
    ct, mean, rhs_part, first_rest, lead, column, weight = stage(
        jnp.reshape(core, (1,)), landmark_fps, fps, sq_norms(fps)[None, :], tgs
    )

    def reduced_pieces(masks):
        starts = []
        for m in masks:
            there = ((layer ^ m) * 4 + core) * share
            starts += [there + row * 2 * share, there + (1 - row) * 2 * share]
        got = pieces(starts, ct, lead, column, rhs_part)
        return [(got[2 * p], got[2 * p + 1]) for p in range(len(masks))]

    def row_sum(pair):
        return pair[0] + send(pair[1], ROW).astype(jnp.float32)

    quarter = share // 4

    def quarter_of(q):
        return lax.dynamic_slice_in_dim(first_rest, (q % 4) * quarter, quarter, 0)

    part = quarter_of(layer).astype(jnp.float32)
    for s in (2, 1, 3):
        part = part + send(quarter_of(layer + s), rotate(s)).astype(jnp.float32)
    part = part.astype(jnp.bfloat16)
    part = part.astype(jnp.float32) + send(part, ROW).astype(jnp.float32)
    part = part.astype(jnp.bfloat16)
    quarters = jnp.zeros((4,) + part.shape, jnp.bfloat16)
    quarters = lax.dynamic_update_index_in_dim(quarters, part, layer, 0)
    for s in (2, 1, 3):
        quarters = lax.dynamic_update_index_in_dim(
            quarters, send(part, rotate(s)), (layer + 4 - s) % 4, 0
        )

    three, two = reduced_pieces((3, 2))
    one, zero = reduced_pieces((1, 0))
    three = row_sum(three).astype(jnp.bfloat16)
    two = row_sum(two) + send(three, NEAR).astype(jnp.float32)
    two = two.astype(jnp.bfloat16)
    one = row_sum(one).astype(jnp.bfloat16)
    own = row_sum(zero) + send(one, NEAR).astype(jnp.float32) + send(two, FAR).astype(jnp.float32)

    stats = gather_chips(jnp.concatenate([mean, target_sum, lead, weight], axis=1))
    means, target_sums = stats[:, :landmarks], stats[:, landmarks : landmarks + LANES]
    leads = stats[:, landmarks + LANES : 2 * landmarks + LANES]
    lead_weights = stats[:, 2 * landmarks + LANES : 2 * landmarks + LANES + 1]
    shift = means - jnp.mean(means, axis=0, keepdims=True)
    left_terms = jnp.concatenate([shift * chip_rows, leads], axis=0)
    right_terms = jnp.concatenate([shift, leads * lead_weights], axis=0)

    def add_back(start):
        return highest(lax.dynamic_slice_in_dim(left_terms, start, share, 1), right_terms)

    block_fps = lax.dynamic_slice_in_dim(landmark_fps, core * share, share, 0)
    block = (quarters.reshape(share, landmarks).astype(jnp.float32) + add_back(core * share)) * scale
    block = block + tanimoto(block_fps, landmark_fps, norms)
    other = send(block, CORE)
    panel_rows = lax.dynamic_slice_in_dim(
        jnp.concatenate([block, other, block], axis=0), core * share, 2 * share, 0
    )
    state = jnp.concatenate([panel_rows[:, :width], jnp.eye(width, dtype=jnp.float32)], axis=1)
    for b in range(0, width // CHOL, 2):
        state = eliminate_blocks(state, (b, b + 1))
    factor = exact_dot(state[:, width:], panel_rows)

    start = position * share
    own_fps = lax.dynamic_slice_in_dim(landmark_fps, start, share, 0)
    rest = (own[:, : landmarks - width] + add_back(start)[:, width:]) * scale + tanimoto(
        own_fps, landmark_fps[width:], norms[width:]
    )
    own_shift = lax.dynamic_slice_in_dim(shift, start, share, 1)
    rhs = (own[:, landmarks - width :] + highest(own_shift, target_sums)) / math.sqrt(
        ridge_weight * total_rows
    )
    own_panel = lax.dynamic_slice_in_dim(panel_rows, start, share, 1)
    own_factor = lax.dynamic_slice_in_dim(factor, start, share, 1)
    system_rows = jnp.concatenate([own_panel.T, rest], axis=1)
    trailing = system_rows - highest(own_factor, factor)
    return (rhs, own_factor.T, trailing)


def solution(mesh):
    local = local_16 if mesh.shape["dp"] == 16 else local_any
    in_specs = (P(("groups", "dp"), None), P(("groups", "dp"), None), P("groups"))
    out_specs = (P(("groups", "dp"), None), P(("groups", "dp"), None), P(("groups", "dp"), None))
    return jax.shard_map(local, mesh=mesh, in_specs=in_specs, out_specs=out_specs, check_vma=False)
```

```python
import functools
import math

import jax
import jax.numpy as jnp
from jax import lax
from jax.experimental import pallas as pl
from jax.experimental.pallas import tpu as pltpu
from jax.sharding import PartitionSpec as P

PB = 256


ridge_weight = 0.01


def sq_norms(row_block):
    wide_rows = row_block.astype(jnp.float32)
    return jnp.sum(wide_rows * wide_rows, axis=1)


def tanimoto(row_block, landmark_fps, landmark_norms):
    inner_prod = lax.dot_general(
        row_block, landmark_fps, (((1,), (1,)), ((), ())), preferred_element_type=jnp.float32
    )
    row_norms = sq_norms(row_block)
    return inner_prod / (row_norms[:, None] + landmark_norms[None, :] - inner_prod)


def local_any(fingerprints, targets, landmark_index):
    rows_dev = fingerprints.shape[0]
    devices = lax.axis_size("dp")
    total_rows = rows_dev * devices
    landmarks = landmark_index.shape[0]
    land_share = landmarks // devices
    position = lax.axis_index("dp")
    owner_dev = landmark_index // rows_dev
    offset = landmark_index % rows_dev
    is_mine = owner_dev == position
    capacity = 2 * land_share
    owner_onehot = (owner_dev[:, None] == jnp.arange(devices, dtype=jnp.int32)[None, :]).astype(
        jnp.int32
    )
    owner_rank = jnp.sum(jnp.cumsum(owner_onehot, axis=0) * owner_onehot, axis=1) - 1
    slot_rows = (
        jnp.zeros((capacity,), jnp.int32)
        .at[jnp.where(is_mine, owner_rank, capacity)]
        .set(offset, mode="drop")
    )
    packed = fingerprints[slot_rows]
    gathered = lax.all_gather(packed, "dp", axis=0, tiled=True)
    landmark_fps = gathered[owner_dev * capacity + owner_rank]
    landmark_norms = sq_norms(landmark_fps)
    kernel = tanimoto(fingerprints, landmark_fps, landmark_norms)
    col_total = lax.psum(jnp.sum(kernel, axis=0), "dp")
    col_mean = col_total / total_rows
    centred = (kernel - col_mean[None, :]).astype(jnp.bfloat16)
    joined = jnp.concatenate([centred, targets], axis=1)
    totals = lax.psum_scatter(
        lax.dot_general(
            centred, joined, (((0,), (0,)), ((), ())), preferred_element_type=jnp.float32
        ),
        "dp",
        scatter_dimension=0,
        tiled=True,
    )
    gram_rows = totals[:, :landmarks]
    rhs_rows = totals[:, landmarks:]
    rhs = rhs_rows / math.sqrt(ridge_weight * total_rows)
    own_fps = lax.dynamic_slice_in_dim(landmark_fps, position * land_share, land_share, 0)
    system_rows = gram_rows / (ridge_weight * total_rows) + tanimoto(
        own_fps, landmark_fps, landmark_norms
    )
    panel_width = PB
    column_block = lax.all_gather(system_rows[:, :panel_width], "dp", axis=0, tiled=True)
    corner = jnp.linalg.cholesky(column_block[:panel_width])
    panel_full = lax.linalg.triangular_solve(
        corner, column_block, left_side=False, lower=True, transpose_a=True
    )
    panel_own = lax.dynamic_slice_in_dim(panel_full, position * land_share, land_share, 0)
    trailing = system_rows - jnp.dot(panel_own, panel_full.T, precision=lax.Precision.HIGHEST)
    return (rhs, panel_own, trailing)


CORE = [(i, i ^ 1) for i in range(16)]
ROW = [(i, i ^ 2) for i in range(16)]
NEAR = [(i, i ^ 4) for i in range(16)]
FAR = [(i, i ^ 8) for i in range(16)]
LANES = 128
TILE = 256
VMEM_BYTES = 56 * 2**20


def rotate(step):
    return [(i, (i + 4 * step) % 16) for i in range(16)]


def send(x, perm):
    return lax.ppermute(x, "dp", perm)


def highest(a, b):
    return lax.dot_general(
        a,
        b,
        (((0,), (0,)), ((), ())),
        precision=lax.Precision.HIGHEST,
        preferred_element_type=jnp.float32,
    )


def dot_nt(a, b):
    return lax.dot_general(a, b, (((1,), (1,)), ((), ())), preferred_element_type=jnp.float32)


def dot_nn(a, b):
    return lax.dot_general(a, b, (((1,), (0,)), ((), ())), preferred_element_type=jnp.float32)


def gather_chips(x):
    pair = jnp.concatenate([x, send(x, ROW)], axis=0)
    return jnp.concatenate([pair] + [send(pair, rotate(s)) for s in (1, 2, 3)], axis=0)


def vmem(count):
    return [pl.BlockSpec(memory_space=pltpu.VMEM)] * count


def spread(row_vector):
    return jnp.broadcast_to(row_vector, (LANES, LANES)).T


def stage_body(
    core_ref, land_ref, fps_ref, norms_ref, tgs_ref,
    ct_ref, mean_ref, rhs_ref, rest_ref, lead_ref, column_ref, weight_ref,
    cent_ref, first_ref,
):
    step = pl.program_id(0)
    rows = fps_ref.shape[0]
    base = pl.multiple_of(step * TILE, TILE)
    block = pl.multiple_of(core_ref[0] * LANES, LANES)
    tile = land_ref[...]
    wide = tile.astype(jnp.float32)
    land_norms = jnp.sum(wide * wide, axis=1, keepdims=True)
    total = jnp.zeros((TILE, 1), jnp.float32)
    for n in range(0, rows, TILE):
        inner = dot_nt(tile, fps_ref[n : n + TILE, :])
        kernel = inner / (norms_ref[:, n : n + TILE] + land_norms - inner)
        cent_ref[:, n : n + TILE] = kernel
        total = total + jnp.sum(kernel, axis=1, keepdims=True)
    mean = total * (1.0 / rows)
    for n in range(0, rows, TILE):
        cent = cent_ref[:, n : n + TILE] - mean
        cent_ref[:, n : n + TILE] = cent
        ct_ref[pl.ds(base, TILE), n : n + TILE] = cent.astype(jnp.bfloat16)
    mean_ref[:, pl.ds(base, TILE)] = jnp.broadcast_to(mean, (TILE, LANES)).T[:1, :]
    own = cent_ref[pl.ds(block, LANES), :]
    high = own.astype(jnp.bfloat16)
    low = (own - high.astype(jnp.float32)).astype(jnp.bfloat16)
    rhs_ref[step] = dot_nn(high, tgs_ref[...]) + dot_nn(low, tgs_ref[...])
    first_ref[:, pl.ds(base, TILE)] = dot_nt(
        ct_ref[pl.ds(block, LANES), :], ct_ref[pl.ds(base, TILE), :]
    )

    @pl.when(step == pl.num_programs(0) - 1)
    def _():
        lead = jnp.sum(first_ref[...], axis=0, keepdims=True)
        lead_ref[...] = lead
        lead_own = lead_ref[:, pl.ds(block, LANES)]
        mass = jnp.sum(lead_own, axis=1, keepdims=True)
        size = jnp.sum(jnp.abs(lead_own), axis=1, keepdims=True)
        usable = mass > 1e-3 * size
        weight = jnp.where(usable, 1.0 / jnp.where(usable, mass, 1.0), 0.0)
        weight_ref[...] = jnp.broadcast_to(weight, (1, LANES))
        mine = spread(lead_own) * weight
        for j in range(lead.shape[1] // LANES):
            cols = slice(j * LANES, (j + 1) * LANES)
            part = lead[:, cols]
            column_ref[cols, :] = spread(part) * weight
            rest_ref[:, cols] = (first_ref[:, cols] - mine * part).astype(jnp.bfloat16)


def stage(core, landmark_fps, fps, norms, tgs):
    rows, length = fps.shape
    landmarks = landmark_fps.shape[0]
    steps = landmarks // TILE
    f32 = jnp.float32

    def whole(shape):
        return pl.BlockSpec(shape, lambda i, c: (0,) * len(shape))

    outs = [
        ((landmarks, rows), jnp.bfloat16),
        ((1, landmarks), f32),
        ((steps, LANES, LANES), f32),
        ((LANES, landmarks), jnp.bfloat16),
        ((1, landmarks), f32),
        ((landmarks, LANES), f32),
        ((1, LANES), f32),
    ]
    return pl.pallas_call(
        stage_body,
        grid_spec=pltpu.PrefetchScalarGridSpec(
            num_scalar_prefetch=1,
            grid=(steps,),
            in_specs=[
                pl.BlockSpec((TILE, length), lambda i, c: (i, 0)),
                whole(fps.shape),
                whole(norms.shape),
                whole(tgs.shape),
            ],
            out_specs=[whole(s) for s, _ in outs],
            scratch_shapes=[
                pltpu.VMEM((TILE, rows), f32),
                pltpu.VMEM((LANES, landmarks), f32),
            ],
        ),
        out_shape=[jax.ShapeDtypeStruct(s, d) for s, d in outs],
        compiler_params=pltpu.CompilerParams(vmem_limit_bytes=VMEM_BYTES),
        name="stage",
    )(core, landmark_fps, fps, norms, tgs)


def pieces_body(at_ref, ct_ref, lead_ref, column_ref, rhs_ref, *refs):
    outs, left_ref = refs[:-1], refs[-1]
    count = len(outs)
    for p in range(count):
        at = pl.multiple_of(at_ref[p], LANES)
        left_ref[p * LANES : (p + 1) * LANES, :] = ct_ref[pl.ds(at, LANES), :]
    for t in range(1, ct_ref.shape[0] // TILE):
        for q in range(0, count, 2):
            got = dot_nt(
                left_ref[q * LANES : (q + 2) * LANES, :], ct_ref[t * TILE : (t + 1) * TILE, :]
            )
            for p in (q, q + 1):
                out = outs[p]
                at = pl.multiple_of(at_ref[p], LANES)
                column = column_ref[pl.ds(at, LANES), :]
                for h in range(TILE // LANES):
                    lo = t * TILE + h * LANES
                    part = got[(p - q) * LANES : (p - q + 1) * LANES, h * LANES : (h + 1) * LANES]
                    part = part - column * lead_ref[:, lo : lo + LANES]
                    out[:, lo - TILE : lo - TILE + LANES] = part.astype(out.dtype)
    for p, out in enumerate(outs):
        out[:, ct_ref.shape[0] - TILE :] = rhs_ref[at_ref[p] // TILE].astype(out.dtype)


def pieces(starts, ct, lead, column, rhs_part):
    width = ct.shape[0] - TILE + LANES
    outs = [jnp.float32, jnp.bfloat16] * (len(starts) // 2)
    return pl.pallas_call(
        pieces_body,
        in_specs=[pl.BlockSpec(memory_space=pltpu.SMEM)] + vmem(4),
        out_specs=vmem(len(outs)),
        out_shape=[jax.ShapeDtypeStruct((LANES, width), d) for d in outs],
        scratch_shapes=[pltpu.VMEM((len(outs) * LANES, ct.shape[1]), jnp.bfloat16)],
        compiler_params=pltpu.CompilerParams(vmem_limit_bytes=VMEM_BYTES),
        name="pieces",
    )(jnp.stack(starts).astype(jnp.int32), ct, lead, column, rhs_part)


CHOL = 32


def exact_dot(a, b, dims=((1,), (0,))):
    return lax.dot_general(
        a, b, (dims, ((), ())), precision=lax.Precision.HIGHEST, preferred_element_type=jnp.float32
    )


def factor_body(blocks, state_ref, out_ref):
    size = state_ref.shape[0]
    out_ref[...] = state_ref[...]
    sub = lax.broadcasted_iota(jnp.int32, (CHOL, LANES), 0)
    lane = lax.broadcasted_iota(jnp.int32, (CHOL, LANES), 1)
    for b in blocks:
        lo, hi = b * CHOL, (b + 1) * CHOL
        diag = out_ref[lo:hi, lo:hi]
        work = jnp.concatenate(
            [
                diag,
                (sub == lane)[:, :CHOL].astype(jnp.float32),
                jnp.zeros((CHOL, LANES - 2 * CHOL), jnp.float32),
            ],
            axis=1,
        )

        for k in range(CHOL):
            col = jnp.broadcast_to(work[:, k : k + 1], work.shape)
            row = work[k : k + 1, :] / col[k : k + 1, :]
            work = work - jnp.where(sub > k, col, 0.0) * row
        pivots = jnp.sum(jnp.where(sub == lane, work, 0.0), axis=1, keepdims=True)
        inverse = work[:, CHOL : 2 * CHOL] / jnp.sqrt(pivots)
        done = exact_dot(inverse, out_ref[lo:hi, :])
        out_ref[lo:hi, :] = done
        if hi < size:
            left = hi // LANES * LANES
            cols = slice(left, size + -(-hi // LANES) * LANES)
            out_ref[hi:, cols] = out_ref[hi:, cols] - exact_dot(
                done[:, hi:size], done[:, cols], ((0,), (0,))
            )


def eliminate_blocks(state, blocks):
    return pl.pallas_call(
        functools.partial(factor_body, blocks),
        in_specs=vmem(1),
        out_specs=vmem(1)[0],
        out_shape=jax.ShapeDtypeStruct(state.shape, jnp.float32),
        compiler_params=pltpu.CompilerParams(vmem_limit_bytes=VMEM_BYTES),
        name="factor",
    )(state)


def pack_body(at_ref, index_ref, fps_ref, packed_ref, slots_ref, key_ref, pick_ref):
    rows, landmarks = fps_ref.shape[0], index_ref.shape[1]
    capacity = packed_ref.shape[0]
    f32 = jnp.float32
    index = index_ref[...].astype(f32)
    owner = jnp.floor(index * (1.0 / rows))
    key_ref[1:2, :] = index - owner * rows
    device = lax.broadcasted_iota(jnp.int32, (16, TILE), 0).astype(f32)
    before = lax.broadcasted_iota(jnp.int32, (TILE, TILE), 0)
    before = (before < lax.broadcasted_iota(jnp.int32, (TILE, TILE), 1)).astype(jnp.bfloat16)
    owners = [owner[:, n : n + TILE] for n in range(0, landmarks, TILE)]
    owned = [(device == o).astype(f32) for o in owners]
    within = dot_nn(jnp.concatenate(owned, axis=0).astype(jnp.bfloat16), before)
    ahead = jnp.zeros((16, 1), f32)
    slot_in = lax.broadcasted_iota(jnp.int32, (capacity, TILE), 0).astype(f32)
    for b, o in enumerate(owners):
        counts = within[b * 16 : (b + 1) * 16, :] + ahead
        rank = jnp.sum(owned[b] * counts, axis=0, keepdims=True)
        ahead = ahead + jnp.sum(owned[b], axis=1, keepdims=True)
        slot = o * capacity + rank
        for h in range(0, TILE, LANES):
            lo = b * TILE + h
            slots_ref[lo : lo + LANES, :] = spread(slot[:, h : h + LANES])
        key = jnp.where(o == at_ref[0].astype(f32), rank, -1.0)
        pick_ref[:, b * TILE : (b + 1) * TILE] = (slot_in == key).astype(jnp.bfloat16)
    packed = jnp.zeros(packed_ref.shape, f32)
    for r in range(0, rows, TILE):
        row_in = lax.broadcasted_iota(jnp.int32, (TILE, landmarks), 0).astype(f32) + r
        here = (row_in == key_ref[1:2, :]).astype(jnp.bfloat16)
        chosen = dot_nt(pick_ref[...], here).astype(jnp.bfloat16)
        packed = packed + dot_nn(chosen, fps_ref[r : r + TILE, :])
    packed_ref[...] = packed.astype(jnp.bfloat16)


def pack(position, landmark_index, fingerprints):
    landmarks = landmark_index.shape[0]
    capacity = landmarks // 8
    return pl.pallas_call(
        pack_body,
        in_specs=[pl.BlockSpec(memory_space=pltpu.SMEM)] + vmem(2),
        out_specs=vmem(2),
        out_shape=[
            jax.ShapeDtypeStruct((capacity, fingerprints.shape[1]), jnp.bfloat16),
            jax.ShapeDtypeStruct((landmarks, LANES), jnp.float32),
        ],
        scratch_shapes=[
            pltpu.VMEM((8, landmarks), jnp.float32),
            pltpu.VMEM((capacity, landmarks), jnp.bfloat16),
        ],
        compiler_params=pltpu.CompilerParams(vmem_limit_bytes=VMEM_BYTES),
        name="pack",
    )(jnp.reshape(position, (1,)), landmark_index[None, :], fingerprints)


def place_body(count, base_ref, slots_ref, *refs):
    chunks, before, out_ref = refs[:count], refs[count:-1], refs[-1]
    slots = slots_ref[...]
    lane = lax.broadcasted_iota(jnp.int32, slots.shape, 1).astype(jnp.float32)
    got = before[0][...].astype(jnp.float32) if before else jnp.zeros(out_ref.shape, jnp.float32)
    for n, chunk in enumerate(chunks):
        inside = slots - base_ref[n].astype(jnp.float32)
        chosen = jnp.concatenate(
            [
                (inside == lane + h).astype(jnp.float32)
                for h in range(0, chunk.shape[0], LANES)
            ],
            axis=1,
        )
        got = got + dot_nn(chosen.astype(jnp.bfloat16), chunk[...])
    out_ref[...] = got.astype(jnp.bfloat16)


def place(owners, chunks, slots, before=None):
    capacity, length = chunks[0].shape
    landmarks = slots.shape[0]
    tile = pl.BlockSpec((TILE, length), lambda i: (i, 0))
    extra = [] if before is None else [before]
    return pl.pallas_call(
        functools.partial(place_body, len(chunks)),
        grid=(landmarks // TILE,),
        in_specs=[
            pl.BlockSpec(memory_space=pltpu.SMEM),
            pl.BlockSpec((TILE, LANES), lambda i: (i, 0)),
        ]
        + [pl.BlockSpec((capacity, length), lambda i: (0, 0))] * len(chunks)
        + [tile] * len(extra),
        out_specs=tile,
        out_shape=jax.ShapeDtypeStruct((landmarks, length), jnp.bfloat16),
        compiler_params=pltpu.CompilerParams(vmem_limit_bytes=VMEM_BYTES),
        name="place",
    )((jnp.stack(owners) * capacity).astype(jnp.int32), slots, *chunks, *extra)


def landmarks_everywhere(fingerprints, landmark_index):
    position = lax.axis_index("dp")
    packed, slots = pack(position, landmark_index, fingerprints)
    held = {0: packed}
    for perm, mask in ((FAR, 8), (NEAR, 4), (ROW, 2)):
        held[mask] = send(packed, perm)
    held[12] = send(held[8], NEAR)
    held[6] = send(held[4], ROW)
    held[10] = send(held[8], ROW)
    held[14] = send(held[12], ROW)
    result = None
    for masks in ((0, 2, 4, 8), (6, 12, 10), (14,)):
        owners, chunks = [], []
        for m in masks:
            owners += [position ^ m, position ^ m ^ 1]
            chunks += [held[m], send(held[m], CORE)]
        result = place(owners, chunks, slots, result)
    return result


def local_16(fingerprints, targets, landmark_index):
    rows_dev = fingerprints.shape[0]
    total_rows = rows_dev * 16
    landmarks = landmark_index.shape[0]
    share = landmarks // 16
    width = PB
    position = lax.axis_index("dp")
    core = position % 2
    row = (position // 2) % 2
    layer = position // 4
    scale = 1.0 / (ridge_weight * total_rows)

    fps = jnp.concatenate([fingerprints, send(fingerprints, CORE)], axis=0)
    tgs = jnp.concatenate([targets, send(targets, CORE)], axis=0)
    chip_rows = 2 * rows_dev
    landmark_fps = landmarks_everywhere(fingerprints, landmark_index)
    norms = sq_norms(landmark_fps)
    target_sum = jnp.sum(tgs.astype(jnp.float32), axis=0, keepdims=True)
    ct, mean, rhs_part, first_rest, lead, column, weight = stage(
        jnp.reshape(core, (1,)), landmark_fps, fps, sq_norms(fps)[None, :], tgs
    )

    def reduced_pieces(masks):
        starts = []
        for m in masks:
            there = ((layer ^ m) * 4 + core) * share
            starts += [there + row * 2 * share, there + (1 - row) * 2 * share]
        got = pieces(starts, ct, lead, column, rhs_part)
        return [(got[2 * p], got[2 * p + 1]) for p in range(len(masks))]

    def row_sum(pair):
        return pair[0] + send(pair[1], ROW).astype(jnp.float32)

    stats = gather_chips(jnp.concatenate([mean, target_sum, lead, weight], axis=1))
    means, target_sums = stats[:, :landmarks], stats[:, landmarks : landmarks + LANES]
    leads = stats[:, landmarks + LANES : 2 * landmarks + LANES]
    lead_weights = stats[:, 2 * landmarks + LANES : 2 * landmarks + LANES + 1]
    shift = means - jnp.mean(means, axis=0, keepdims=True)
    left_terms = jnp.concatenate([shift * chip_rows, leads], axis=0)
    right_terms = jnp.concatenate([shift, leads * lead_weights], axis=0)

    def system_part(sums, start, cols):
        rows_fps = lax.dynamic_slice_in_dim(landmark_fps, start, share, 0)
        terms = lax.dynamic_slice_in_dim(left_terms, start, share, 1)
        return (sums + highest(terms, right_terms[:, cols])) * scale + tanimoto(
            rows_fps, landmark_fps[cols], norms[cols]
        )

    def both_blocks(block):
        other = send(block, CORE)
        return lax.dynamic_slice_in_dim(
            jnp.concatenate([block, other, block], axis=0), core * share, 2 * share, 0
        )

    panel_cols, other_cols = slice(0, width), slice(width, landmarks)
    corner = first_rest[:, panel_cols]
    corner = corner.astype(jnp.float32) + send(corner, ROW).astype(jnp.float32)
    half = corner.astype(jnp.bfloat16)
    for s in (2, 1, 3):
        corner = corner + send(half, rotate(s)).astype(jnp.float32)
    corner = both_blocks(system_part(corner, core * share, panel_cols))
    state = jnp.concatenate([corner, jnp.eye(width, dtype=jnp.float32)], axis=1)
    for b in range(0, width // CHOL, 2):
        state = eliminate_blocks(state, (b, b + 1))

    first_rest = first_rest[:, other_cols]
    quarter = share // 4

    def quarter_of(q):
        return lax.dynamic_slice_in_dim(first_rest, (q % 4) * quarter, quarter, 0)

    part = quarter_of(layer).astype(jnp.float32)
    for s in (2, 1, 3):
        part = part + send(quarter_of(layer + s), rotate(s)).astype(jnp.float32)
    part = part.astype(jnp.bfloat16)
    part = part.astype(jnp.float32) + send(part, ROW).astype(jnp.float32)
    part = part.astype(jnp.bfloat16)
    quarters = jnp.zeros((4,) + part.shape, jnp.bfloat16)
    quarters = lax.dynamic_update_index_in_dim(quarters, part, layer, 0)
    for s in (2, 1, 3):
        quarters = lax.dynamic_update_index_in_dim(
            quarters, send(part, rotate(s)), (layer + 4 - s) % 4, 0
        )
    block = system_part(
        quarters.reshape(share, landmarks - width).astype(jnp.float32), core * share, other_cols
    )
    panel_rows = jnp.concatenate([corner, both_blocks(block)], axis=1)
    factor = exact_dot(state[:, width:], panel_rows)

    three, two = reduced_pieces((3, 2))
    one, zero = reduced_pieces((1, 0))
    three = row_sum(three).astype(jnp.bfloat16)
    two = row_sum(two) + send(three, NEAR).astype(jnp.float32)
    two = two.astype(jnp.bfloat16)
    one = row_sum(one).astype(jnp.bfloat16)
    own = row_sum(zero) + send(one, NEAR).astype(jnp.float32) + send(two, FAR).astype(jnp.float32)

    start = position * share
    rest = system_part(own[:, : landmarks - width], start, other_cols)
    own_shift = lax.dynamic_slice_in_dim(shift, start, share, 1)
    rhs = (own[:, landmarks - width :] + highest(own_shift, target_sums)) / math.sqrt(
        ridge_weight * total_rows
    )
    own_panel = lax.dynamic_slice_in_dim(panel_rows, start, share, 1)
    own_factor = lax.dynamic_slice_in_dim(factor, start, share, 1)
    system_rows = jnp.concatenate([own_panel.T, rest], axis=1)
    trailing = system_rows - highest(own_factor, factor)
    return (rhs, own_factor.T, trailing)


def solution(mesh):
    local = local_16 if mesh.shape["dp"] == 16 else local_any
    in_specs = (P(("groups", "dp"), None), P(("groups", "dp"), None), P("groups"))
    out_specs = (P(("groups", "dp"), None), P(("groups", "dp"), None), P(("groups", "dp"), None))
    return jax.shard_map(local, mesh=mesh, in_specs=in_specs, out_specs=out_specs, check_vma=False)
```

```python
import functools
import math

import jax
import jax.numpy as jnp
from jax import lax
from jax.experimental import pallas as pl
from jax.experimental.pallas import tpu as pltpu
from jax.sharding import PartitionSpec as P

PB = 256


ridge_weight = 0.01


def sq_norms(row_block):
    wide_rows = row_block.astype(jnp.float32)
    return jnp.sum(wide_rows * wide_rows, axis=1)


def tanimoto(row_block, landmark_fps, landmark_norms):
    inner_prod = lax.dot_general(
        row_block, landmark_fps, (((1,), (1,)), ((), ())), preferred_element_type=jnp.float32
    )
    row_norms = sq_norms(row_block)
    return inner_prod / (row_norms[:, None] + landmark_norms[None, :] - inner_prod)


def local_any(fingerprints, targets, landmark_index):
    rows_dev = fingerprints.shape[0]
    devices = lax.axis_size("dp")
    total_rows = rows_dev * devices
    landmarks = landmark_index.shape[0]
    land_share = landmarks // devices
    position = lax.axis_index("dp")
    owner_dev = landmark_index // rows_dev
    offset = landmark_index % rows_dev
    is_mine = owner_dev == position
    capacity = 2 * land_share
    owner_onehot = (owner_dev[:, None] == jnp.arange(devices, dtype=jnp.int32)[None, :]).astype(
        jnp.int32
    )
    owner_rank = jnp.sum(jnp.cumsum(owner_onehot, axis=0) * owner_onehot, axis=1) - 1
    slot_rows = (
        jnp.zeros((capacity,), jnp.int32)
        .at[jnp.where(is_mine, owner_rank, capacity)]
        .set(offset, mode="drop")
    )
    packed = fingerprints[slot_rows]
    gathered = lax.all_gather(packed, "dp", axis=0, tiled=True)
    landmark_fps = gathered[owner_dev * capacity + owner_rank]
    landmark_norms = sq_norms(landmark_fps)
    kernel = tanimoto(fingerprints, landmark_fps, landmark_norms)
    col_total = lax.psum(jnp.sum(kernel, axis=0), "dp")
    col_mean = col_total / total_rows
    centred = (kernel - col_mean[None, :]).astype(jnp.bfloat16)
    joined = jnp.concatenate([centred, targets], axis=1)
    totals = lax.psum_scatter(
        lax.dot_general(
            centred, joined, (((0,), (0,)), ((), ())), preferred_element_type=jnp.float32
        ),
        "dp",
        scatter_dimension=0,
        tiled=True,
    )
    gram_rows = totals[:, :landmarks]
    rhs_rows = totals[:, landmarks:]
    rhs = rhs_rows / math.sqrt(ridge_weight * total_rows)
    own_fps = lax.dynamic_slice_in_dim(landmark_fps, position * land_share, land_share, 0)
    system_rows = gram_rows / (ridge_weight * total_rows) + tanimoto(
        own_fps, landmark_fps, landmark_norms
    )
    panel_width = PB
    column_block = lax.all_gather(system_rows[:, :panel_width], "dp", axis=0, tiled=True)
    corner = jnp.linalg.cholesky(column_block[:panel_width])
    panel_full = lax.linalg.triangular_solve(
        corner, column_block, left_side=False, lower=True, transpose_a=True
    )
    panel_own = lax.dynamic_slice_in_dim(panel_full, position * land_share, land_share, 0)
    trailing = system_rows - jnp.dot(panel_own, panel_full.T, precision=lax.Precision.HIGHEST)
    return (rhs, panel_own, trailing)


CORE = [(i, i ^ 1) for i in range(16)]
ROW = [(i, i ^ 2) for i in range(16)]
NEAR = [(i, i ^ 4) for i in range(16)]
FAR = [(i, i ^ 8) for i in range(16)]
LANES = 128
TILE = 256
MIB = 2**20


def send(x, perm):
    return lax.ppermute(x, "dp", perm)


def highest(a, b):
    return lax.dot_general(
        a,
        b,
        (((0,), (0,)), ((), ())),
        precision=lax.Precision.HIGHEST,
        preferred_element_type=jnp.float32,
    )


def dot_nt(a, b):
    return lax.dot_general(a, b, (((1,), (1,)), ((), ())), preferred_element_type=jnp.float32)


def dot_nn(a, b):
    return lax.dot_general(a, b, (((1,), (0,)), ((), ())), preferred_element_type=jnp.float32)


def after(x, *earlier):
    return lax.optimization_barrier((x,) + earlier)[0]


def vmem(count):
    return [pl.BlockSpec(memory_space=pltpu.VMEM)] * count


def spread(row_vector):
    return jnp.broadcast_to(row_vector, (LANES, LANES)).T


def stage_body(
    core_ref, land_ref, fps_ref, norms_ref, tgs_ref,
    ct_ref, rhs_ref, rest_ref, message_ref, lead_ref, column_ref,
    cent_ref, first_ref, left_ref, low_ref, mean_ref,
):
    step = pl.program_id(0)
    rows = fps_ref.shape[0]
    base = pl.multiple_of(step * TILE, TILE)
    block = pl.multiple_of(core_ref[0] * LANES, LANES)
    tile = land_ref[...]
    wide = tile.astype(jnp.float32)
    land_norms = jnp.sum(wide * wide, axis=1, keepdims=True)
    total = jnp.zeros((TILE, 1), jnp.float32)
    for n in range(0, rows, TILE):
        inner = dot_nt(tile, fps_ref[n : n + TILE, :])
        kernel = inner / (norms_ref[:, n : n + TILE] + land_norms - inner)
        cent_ref[:, n : n + TILE] = kernel
        total = total + jnp.sum(kernel, axis=1, keepdims=True)
    mean = total * (1.0 / rows)
    for n in range(0, rows, TILE):
        cent = cent_ref[:, n : n + TILE] - mean
        high = cent.astype(jnp.bfloat16)
        ct_ref[:, n : n + TILE] = high
        low_ref[:, n : n + TILE] = (cent - high.astype(jnp.float32)).astype(jnp.bfloat16)
    mean_ref[:, pl.ds(base, TILE)] = jnp.broadcast_to(mean, (TILE, LANES)).T[:1, :]

    @pl.when(step == 0)
    def _():
        left_ref[:LANES, :] = ct_ref[pl.ds(block, LANES), :]
        left_ref[LANES:, :] = tgs_ref[...]

    both = dot_nt(left_ref[...], ct_ref[...])
    first_ref[:, pl.ds(base, TILE)] = both[:LANES, :]
    cent_ref[:LANES, :TILE] = both[LANES:, :] + dot_nt(left_ref[LANES:, :], low_ref[...])
    rhs_ref[step] = cent_ref[:LANES, pl.ds(block, LANES)].T

    @pl.when(step == pl.num_programs(0) - 1)
    def _():
        lead = jnp.sum(first_ref[...], axis=0, keepdims=True)
        lead_ref[...] = lead
        lead_own = lead_ref[:, pl.ds(block, LANES)]
        mass = jnp.sum(lead_own, axis=1, keepdims=True)
        size = jnp.sum(jnp.abs(lead_own), axis=1, keepdims=True)
        usable = mass > 1e-3 * size
        weight = jnp.where(usable, 1.0 / jnp.where(usable, mass, 1.0), 0.0)
        mine = spread(lead_own) * weight
        for j in range(lead.shape[1] // LANES):
            cols = slice(j * LANES, (j + 1) * LANES)
            part = lead[:, cols]
            column_ref[cols, :] = spread(part) * weight
            rest = first_ref[:, cols] - mine * part
            if j < TILE // LANES:
                message_ref[:LANES, cols] = rest
            else:
                rest_ref[:, slice(cols.start - TILE, cols.stop - TILE)] = rest.astype(jnp.bfloat16)
        message_ref[LANES:, :] = jnp.zeros((message_ref.shape[0] - LANES, TILE), jnp.float32)
        for j in range(lead.shape[1] // TILE):
            cols = slice(j * TILE, (j + 1) * TILE)
            message_ref[LANES + j : LANES + j + 1, :] = mean_ref[:, cols]
            message_ref[LANES + 8 + j : LANES + 9 + j, :] = lead[:, cols]
        at = LANES + 16
        message_ref[at : at + 1, :LANES] = jnp.broadcast_to(weight, (1, LANES))
        sums = jnp.sum(tgs_ref[...].astype(jnp.float32), axis=1, keepdims=True)
        message_ref[at : at + 1, LANES:] = jnp.broadcast_to(sums, (LANES, LANES)).T[:1, :]


STATS = 24


def stage(core, landmark_fps, fps, norms, tgs):
    rows, length = fps.shape
    landmarks = landmark_fps.shape[0]
    steps = landmarks // TILE
    f32, bf16 = jnp.float32, jnp.bfloat16

    def whole(shape):
        return pl.BlockSpec(shape, lambda i, c: (0,) * len(shape))

    outs = [
        ((steps, LANES, LANES), f32),
        ((LANES, landmarks - TILE), bf16),
        ((LANES + STATS, TILE), f32),
        ((1, landmarks), f32),
        ((landmarks, LANES), f32),
    ]
    return pl.pallas_call(
        stage_body,
        grid_spec=pltpu.PrefetchScalarGridSpec(
            num_scalar_prefetch=1,
            grid=(steps,),
            in_specs=[
                pl.BlockSpec((TILE, length), lambda i, c: (i, 0)),
                whole(fps.shape),
                whole(norms.shape),
                whole(tgs.shape),
            ],
            out_specs=[pl.BlockSpec((TILE, rows), lambda i, c: (i, 0))]
            + [whole(s) for s, _ in outs],
            scratch_shapes=[
                pltpu.VMEM((TILE, rows), f32),
                pltpu.VMEM((LANES, landmarks), f32),
                pltpu.VMEM((2 * LANES, rows), bf16),
                pltpu.VMEM((TILE, rows), bf16),
                pltpu.VMEM((1, landmarks), f32),
            ],
        ),
        out_shape=[jax.ShapeDtypeStruct((landmarks, rows), bf16)]
        + [jax.ShapeDtypeStruct(s, d) for s, d in outs],
        compiler_params=pltpu.CompilerParams(vmem_limit_bytes=28 * MIB),
        name="stage",
    )(core, landmark_fps, fps, norms, tgs)


def pieces_body(at_ref, ct_ref, lead_ref, column_ref, rhs_ref, mine_ref, theirs_ref, left_ref):
    count = left_ref.shape[0] // LANES
    for p in range(count):
        at = pl.multiple_of(at_ref[p], LANES)
        left_ref[p * LANES : (p + 1) * LANES, :] = ct_ref[pl.ds(at, LANES), :]

    def store(p, cols, value):
        out = (mine_ref, theirs_ref)[p % 2]
        out[p // 2 * LANES : (p // 2 + 1) * LANES, cols] = value.astype(out.dtype)

    for t in range(1, ct_ref.shape[0] // TILE):
        for q in range(0, count, 2):
            got = dot_nt(
                left_ref[q * LANES : (q + 2) * LANES, :], ct_ref[t * TILE : (t + 1) * TILE, :]
            )
            for p in (q, q + 1):
                at = pl.multiple_of(at_ref[p], LANES)
                column = column_ref[pl.ds(at, LANES), :]
                for h in range(TILE // LANES):
                    lo = t * TILE + h * LANES
                    part = got[(p - q) * LANES : (p - q + 1) * LANES, h * LANES : (h + 1) * LANES]
                    part = part - column * lead_ref[:, lo : lo + LANES]
                    store(p, slice(lo - TILE, lo - TILE + LANES), part)
    for p in range(count):
        lo = ct_ref.shape[0] - TILE
        store(p, slice(lo, lo + LANES), rhs_ref[at_ref[p] // TILE])


def pieces(starts, ct, lead, column, rhs_part):
    shape = (len(starts) // 2 * LANES, ct.shape[0] - TILE + LANES)
    return pl.pallas_call(
        pieces_body,
        in_specs=[pl.BlockSpec(memory_space=pltpu.SMEM)] + vmem(4),
        out_specs=vmem(2),
        out_shape=[
            jax.ShapeDtypeStruct(shape, jnp.float32),
            jax.ShapeDtypeStruct(shape, jnp.bfloat16),
        ],
        scratch_shapes=[pltpu.VMEM((2 * shape[0], ct.shape[1]), jnp.bfloat16)],
        compiler_params=pltpu.CompilerParams(vmem_limit_bytes=28 * MIB),
        name="pieces",
    )(jnp.stack(starts).astype(jnp.int32), ct, lead, column, rhs_part)


CHOL = 32


def exact_dot(a, b, dims=((1,), (0,))):
    return lax.dot_general(
        a, b, (dims, ((), ())), precision=lax.Precision.HIGHEST, preferred_element_type=jnp.float32
    )


def factor_body(blocks, state_ref, out_ref):
    size = state_ref.shape[0]
    out_ref[...] = state_ref[...]
    sub = lax.broadcasted_iota(jnp.int32, (CHOL, LANES), 0)
    lane = lax.broadcasted_iota(jnp.int32, (CHOL, LANES), 1)
    for b in blocks:
        lo, hi = b * CHOL, (b + 1) * CHOL
        diag = out_ref[lo:hi, lo:hi]
        work = jnp.concatenate(
            [
                diag,
                (sub == lane)[:, :CHOL].astype(jnp.float32),
                jnp.zeros((CHOL, LANES - 2 * CHOL), jnp.float32),
            ],
            axis=1,
        )

        for k in range(CHOL):
            col = jnp.broadcast_to(work[:, k : k + 1], work.shape)
            row = work[k : k + 1, :] / col[k : k + 1, :]
            work = work - jnp.where(sub > k, col, 0.0) * row
        pivots = jnp.sum(jnp.where(sub == lane, work, 0.0), axis=1, keepdims=True)
        inverse = work[:, CHOL : 2 * CHOL] / jnp.sqrt(pivots)
        done = exact_dot(inverse, out_ref[lo:hi, :])
        out_ref[lo:hi, :] = done
        if hi < size:
            left = hi // LANES * LANES
            cols = slice(left, size + -(-hi // LANES) * LANES)
            out_ref[hi:, cols] = out_ref[hi:, cols] - exact_dot(
                done[:, hi:size], done[:, cols], ((0,), (0,))
            )


def eliminate_blocks(state, blocks):
    return pl.pallas_call(
        functools.partial(factor_body, blocks),
        in_specs=vmem(1),
        out_specs=vmem(1)[0],
        out_shape=jax.ShapeDtypeStruct(state.shape, jnp.float32),
        compiler_params=pltpu.CompilerParams(vmem_limit_bytes=28 * MIB),
        name="factor",
    )(state)


def pack_body(at_ref, index_ref, fps_ref, packed_ref, slots_ref, key_ref, pick_ref):
    rows, landmarks = fps_ref.shape[0], index_ref.shape[1]
    capacity = packed_ref.shape[0]
    f32 = jnp.float32
    index = index_ref[...].astype(f32)
    owner = jnp.floor(index * (1.0 / rows))
    key_ref[1:2, :] = index - owner * rows
    device = lax.broadcasted_iota(jnp.int32, (16, TILE), 0).astype(f32)
    before = lax.broadcasted_iota(jnp.int32, (TILE, TILE), 0)
    before = (before < lax.broadcasted_iota(jnp.int32, (TILE, TILE), 1)).astype(jnp.bfloat16)
    owners = [owner[:, n : n + TILE] for n in range(0, landmarks, TILE)]
    owned = [(device == o).astype(f32) for o in owners]
    within = dot_nn(jnp.concatenate(owned, axis=0).astype(jnp.bfloat16), before)
    ahead = jnp.zeros((16, 1), f32)
    slot_in = lax.broadcasted_iota(jnp.int32, (capacity, TILE), 0).astype(f32)
    for b, o in enumerate(owners):
        counts = within[b * 16 : (b + 1) * 16, :] + ahead
        rank = jnp.sum(owned[b] * counts, axis=0, keepdims=True)
        ahead = ahead + jnp.sum(owned[b], axis=1, keepdims=True)
        slot = o * capacity + rank
        for h in range(0, TILE, LANES):
            lo = b * TILE + h
            slots_ref[lo : lo + LANES, :] = spread(slot[:, h : h + LANES])
        key = jnp.where(o == at_ref[0].astype(f32), rank, -1.0)
        pick_ref[:, b * TILE : (b + 1) * TILE] = (slot_in == key).astype(jnp.bfloat16)
    packed = jnp.zeros(packed_ref.shape, f32)
    for r in range(0, rows, TILE):
        row_in = lax.broadcasted_iota(jnp.int32, (TILE, landmarks), 0).astype(f32) + r
        here = (row_in == key_ref[1:2, :]).astype(jnp.bfloat16)
        chosen = dot_nt(pick_ref[...], here).astype(jnp.bfloat16)
        packed = packed + dot_nn(chosen, fps_ref[r : r + TILE, :])
    packed_ref[...] = packed.astype(jnp.bfloat16)


def pack(position, landmark_index, fingerprints):
    landmarks = landmark_index.shape[0]
    capacity = landmarks // 8
    return pl.pallas_call(
        pack_body,
        in_specs=[pl.BlockSpec(memory_space=pltpu.SMEM)] + vmem(2),
        out_specs=vmem(2),
        out_shape=[
            jax.ShapeDtypeStruct((capacity, fingerprints.shape[1]), jnp.bfloat16),
            jax.ShapeDtypeStruct((landmarks, LANES), jnp.float32),
        ],
        scratch_shapes=[
            pltpu.VMEM((8, landmarks), jnp.float32),
            pltpu.VMEM((capacity, landmarks), jnp.bfloat16),
        ],
        compiler_params=pltpu.CompilerParams(vmem_limit_bytes=28 * MIB),
        name="pack",
    )(jnp.reshape(position, (1,)), landmark_index[None, :], fingerprints)


def place_body(count, base_ref, slots_ref, *refs):
    chunks, before, out_ref = refs[:count], refs[count:-1], refs[-1]
    slots = slots_ref[...]
    lane = lax.broadcasted_iota(jnp.int32, slots.shape, 1).astype(jnp.float32)
    got = before[0][...].astype(jnp.float32) if before else jnp.zeros(out_ref.shape, jnp.float32)
    for n, chunk in enumerate(chunks):
        inside = slots - base_ref[n].astype(jnp.float32)
        chosen = jnp.concatenate(
            [
                (inside == lane + h).astype(jnp.float32)
                for h in range(0, chunk.shape[0], LANES)
            ],
            axis=1,
        )
        got = got + dot_nn(chosen.astype(jnp.bfloat16), chunk[...])
    out_ref[...] = got.astype(jnp.bfloat16)


def place(owners, chunks, slots, before=None):
    capacity, length = chunks[0].shape
    landmarks = slots.shape[0]
    tile = pl.BlockSpec((TILE, length), lambda i: (i, 0))
    extra = [] if before is None else [before]
    return pl.pallas_call(
        functools.partial(place_body, len(chunks)),
        grid=(landmarks // TILE,),
        in_specs=[
            pl.BlockSpec(memory_space=pltpu.SMEM),
            pl.BlockSpec((TILE, LANES), lambda i: (i, 0)),
        ]
        + [pl.BlockSpec((capacity, length), lambda i: (0, 0))] * len(chunks)
        + [tile] * len(extra),
        out_specs=tile,
        out_shape=jax.ShapeDtypeStruct((landmarks, length), jnp.bfloat16),
        compiler_params=pltpu.CompilerParams(vmem_limit_bytes=28 * MIB),
        name="place",
    )((jnp.stack(owners) * capacity).astype(jnp.int32), slots, *chunks, *extra)


def landmarks_everywhere(fingerprints, landmark_index):
    position = lax.axis_index("dp")
    packed, slots = pack(position, landmark_index, fingerprints)
    held = {0: packed}
    for perm, mask in ((FAR, 8), (NEAR, 4), (ROW, 2)):
        held[mask] = send(packed, perm)
    held[12] = send(held[8], NEAR)
    held[6] = send(held[4], ROW)
    held[10] = send(held[8], ROW)
    held[14] = send(held[12], ROW)
    result = None
    for masks in ((0, 2, 4, 8), (6, 12, 10), (14,)):
        owners, chunks = [], []
        for m in masks:
            owners += [position ^ m, position ^ m ^ 1]
            chunks += [held[m], send(held[m], CORE)]
        result = place(owners, chunks, slots, result)
    return result


def local_16(fingerprints, targets, landmark_index):
    rows_dev = fingerprints.shape[0]
    total_rows = rows_dev * 16
    landmarks = landmark_index.shape[0]
    share = landmarks // 16
    width = PB
    position = lax.axis_index("dp")
    core = position % 2
    row = (position // 2) % 2
    layer = position // 4
    scale = 1.0 / (ridge_weight * total_rows)

    fps = jnp.concatenate([fingerprints, send(fingerprints, CORE)], axis=0)
    tgs = jnp.concatenate([targets, send(targets, CORE)], axis=0)
    chip_rows = 2 * rows_dev
    landmark_fps = landmarks_everywhere(fingerprints, landmark_index)
    norms = sq_norms(landmark_fps)
    ct, rhs_part, rest_rows, message, lead, column = stage(
        jnp.reshape(core, (1,)), landmark_fps, fps, sq_norms(fps)[None, :], tgs.T
    )
    panel_cols, other_cols = slice(0, width), slice(width, landmarks)
    f32, bf16 = jnp.float32, jnp.bfloat16

    def gram_rows(masks, ct):
        starts = []
        for m in masks:
            there = ((layer ^ m) * 4 + core) * share
            starts += [there + row * 2 * share, there + (1 - row) * 2 * share]
        return pieces(starts, ct, lead, column, rhs_part)

    mine_32, theirs_32 = gram_rows((3, 2), ct)
    other_32 = send(theirs_32, ROW)

    def halves(x, high):
        return lax.dynamic_slice_in_dim(x, high * (x.shape[0] // 2), x.shape[0] // 2, 0)

    near, far = layer % 2, layer // 2
    message_row = send(message, ROW)
    other_near = send(halves(rest_rows, 1 - near), NEAR)

    mine_10, theirs_10 = gram_rows((1, 0), ct)
    other_10 = send(theirs_10, ROW)

    def merge(x, y):
        return jnp.concatenate([x[:share] + y[:share], x[share:], y[share:]], axis=0)

    message = merge(message, after(message_row, mine_10))
    message = merge(message, send(message, NEAR))
    part = halves(rest_rows, near).astype(f32) + other_near.astype(f32)
    part_bf = part.astype(bf16)
    message_far = send(message, FAR)
    part = halves(part, far) + send(halves(part_bf, 1 - far), FAR).astype(f32)
    part = part.astype(bf16)
    message = merge(message, message_far)
    part = (part.astype(f32) + send(part, ROW).astype(f32)).astype(bf16)
    part_far = send(part, FAR)

    stats = message[share:].reshape(8, STATS, TILE)
    means = stats[:, :8].reshape(8, landmarks)
    leads = stats[:, 8:16].reshape(8, landmarks)
    lead_weights, target_sums = stats[:, 16, :1], stats[:, 16, LANES:]
    shift = means - jnp.mean(means, axis=0, keepdims=True)
    left_terms = jnp.concatenate([shift * chip_rows, leads], axis=0)
    right_terms = jnp.concatenate([shift, leads * lead_weights], axis=0)

    def system_part(sums, start, cols):
        rows_fps = lax.dynamic_slice_in_dim(landmark_fps, start, share, 0)
        terms = lax.dynamic_slice_in_dim(left_terms, start, share, 1)
        return (sums + highest(terms, right_terms[:, cols])) * scale + tanimoto(
            rows_fps, landmark_fps[cols], norms[cols]
        )

    def in_order(x, other, high):
        size = x.shape[0]
        return lax.dynamic_slice_in_dim(
            jnp.concatenate([x, other, x], axis=0), high * size, 2 * size, 0
        )

    def both_blocks(block):
        return in_order(block, send(block, CORE), core)

    corner = both_blocks(system_part(message[:share], core * share, panel_cols))
    state = jnp.concatenate([corner, jnp.eye(width, dtype=f32)], axis=1)

    sums_32 = mine_32 + other_32.astype(f32)
    three = sums_32[:share].astype(bf16)
    other_two = send(three, NEAR)
    calls = [(b, b + 1) for b in range(0, width // CHOL, 2)]
    state = eliminate_blocks(after(state, three, part_far), calls[0])
    part = in_order(part, part_far, far)
    part_near = send(part, NEAR)
    two = (sums_32[share:] + other_two.astype(f32)).astype(bf16)
    state = eliminate_blocks(after(state, two, part), calls[1])
    got_two = send(two, FAR)
    sums_10 = mine_10 + other_10.astype(f32)
    one = sums_10[:share].astype(bf16)
    got_one = send(one, NEAR)
    state = eliminate_blocks(after(state, one), calls[2])
    part = in_order(part, part_near, near)
    block = both_blocks(system_part(part.astype(f32), core * share, other_cols))
    state = eliminate_blocks(after(state, block), calls[3])
    panel_rows = jnp.concatenate([corner, block], axis=1)
    factor = exact_dot(state[:, width:], panel_rows)

    own = sums_10[share:] + got_one.astype(f32) + got_two.astype(f32)
    start = position * share
    rest = system_part(own[:, : landmarks - width], start, other_cols)
    own_shift = lax.dynamic_slice_in_dim(shift, start, share, 1)
    rhs = (own[:, landmarks - width :] + highest(own_shift, target_sums)) / math.sqrt(
        ridge_weight * total_rows
    )
    own_panel = lax.dynamic_slice_in_dim(panel_rows, start, share, 1)
    own_factor = lax.dynamic_slice_in_dim(factor, start, share, 1)
    system_rows = jnp.concatenate([own_panel.T, rest], axis=1)
    trailing = system_rows - highest(own_factor, factor)
    return (rhs, own_factor.T, trailing)


def solution(mesh):
    local = local_16 if mesh.shape["dp"] == 16 else local_any
    in_specs = (P(("groups", "dp"), None), P(("groups", "dp"), None), P("groups"))
    out_specs = (P(("groups", "dp"), None), P(("groups", "dp"), None), P(("groups", "dp"), None))
    return jax.shard_map(local, mesh=mesh, in_specs=in_specs, out_specs=out_specs, check_vma=False)
```

```python
import functools
import math

import jax
import jax.numpy as jnp
from jax import lax
from jax.experimental import pallas as pl
from jax.experimental.pallas import tpu as pltpu
from jax.sharding import PartitionSpec as P

PB = 256


ridge_weight = 0.01


def sq_norms(row_block):
    wide_rows = row_block.astype(jnp.float32)
    return jnp.sum(wide_rows * wide_rows, axis=1)


def tanimoto(row_block, landmark_fps, landmark_norms):
    inner_prod = lax.dot_general(
        row_block, landmark_fps, (((1,), (1,)), ((), ())), preferred_element_type=jnp.float32
    )
    row_norms = sq_norms(row_block)
    return inner_prod / (row_norms[:, None] + landmark_norms[None, :] - inner_prod)


def local_any(fingerprints, targets, landmark_index):
    rows_dev = fingerprints.shape[0]
    devices = lax.axis_size("dp")
    total_rows = rows_dev * devices
    landmarks = landmark_index.shape[0]
    land_share = landmarks // devices
    position = lax.axis_index("dp")
    owner_dev = landmark_index // rows_dev
    offset = landmark_index % rows_dev
    is_mine = owner_dev == position
    capacity = 2 * land_share
    owner_onehot = (owner_dev[:, None] == jnp.arange(devices, dtype=jnp.int32)[None, :]).astype(
        jnp.int32
    )
    owner_rank = jnp.sum(jnp.cumsum(owner_onehot, axis=0) * owner_onehot, axis=1) - 1
    slot_rows = (
        jnp.zeros((capacity,), jnp.int32)
        .at[jnp.where(is_mine, owner_rank, capacity)]
        .set(offset, mode="drop")
    )
    packed = fingerprints[slot_rows]
    gathered = lax.all_gather(packed, "dp", axis=0, tiled=True)
    landmark_fps = gathered[owner_dev * capacity + owner_rank]
    landmark_norms = sq_norms(landmark_fps)
    kernel = tanimoto(fingerprints, landmark_fps, landmark_norms)
    col_total = lax.psum(jnp.sum(kernel, axis=0), "dp")
    col_mean = col_total / total_rows
    centred = (kernel - col_mean[None, :]).astype(jnp.bfloat16)
    joined = jnp.concatenate([centred, targets], axis=1)
    totals = lax.psum_scatter(
        lax.dot_general(
            centred, joined, (((0,), (0,)), ((), ())), preferred_element_type=jnp.float32
        ),
        "dp",
        scatter_dimension=0,
        tiled=True,
    )
    gram_rows = totals[:, :landmarks]
    rhs_rows = totals[:, landmarks:]
    rhs = rhs_rows / math.sqrt(ridge_weight * total_rows)
    own_fps = lax.dynamic_slice_in_dim(landmark_fps, position * land_share, land_share, 0)
    system_rows = gram_rows / (ridge_weight * total_rows) + tanimoto(
        own_fps, landmark_fps, landmark_norms
    )
    panel_width = PB
    column_block = lax.all_gather(system_rows[:, :panel_width], "dp", axis=0, tiled=True)
    corner = jnp.linalg.cholesky(column_block[:panel_width])
    panel_full = lax.linalg.triangular_solve(
        corner, column_block, left_side=False, lower=True, transpose_a=True
    )
    panel_own = lax.dynamic_slice_in_dim(panel_full, position * land_share, land_share, 0)
    trailing = system_rows - jnp.dot(panel_own, panel_full.T, precision=lax.Precision.HIGHEST)
    return (rhs, panel_own, trailing)


CORE = [(i, i ^ 1) for i in range(16)]
ROW = [(i, i ^ 2) for i in range(16)]
NEAR = [(i, i ^ 4) for i in range(16)]
FAR = [(i, i ^ 8) for i in range(16)]
LANES = 128
TILE = 256
MIB = 2**20


def send(x, perm):
    return lax.ppermute(x, "dp", perm)


def highest(a, b):
    return lax.dot_general(
        a,
        b,
        (((0,), (0,)), ((), ())),
        precision=lax.Precision.HIGHEST,
        preferred_element_type=jnp.float32,
    )


def dot_nt(a, b):
    return lax.dot_general(a, b, (((1,), (1,)), ((), ())), preferred_element_type=jnp.float32)


def dot_nn(a, b):
    return lax.dot_general(a, b, (((1,), (0,)), ((), ())), preferred_element_type=jnp.float32)


def after(x, *earlier):
    return lax.optimization_barrier((x,) + earlier)[0]


def vmem(count):
    return [pl.BlockSpec(memory_space=pltpu.VMEM)] * count


def spread(row_vector):
    return jnp.broadcast_to(row_vector, (LANES, LANES)).T


def stage_body(
    core_ref, land_ref, fps_ref, norms_ref, tgs_ref,
    ct_ref, rhs_ref, rest_ref, message_ref, lead_ref, column_ref,
    cent_ref, first_ref, left_ref, low_ref, mean_ref,
):
    step = pl.program_id(0)
    rows = fps_ref.shape[0]
    base = pl.multiple_of(step * TILE, TILE)
    block = pl.multiple_of(core_ref[0] * LANES, LANES)
    tile = land_ref[...]
    wide = tile.astype(jnp.float32)
    land_norms = jnp.sum(wide * wide, axis=1, keepdims=True)
    total = jnp.zeros((TILE, 1), jnp.float32)
    for n in range(0, rows, TILE):
        inner = dot_nt(tile, fps_ref[n : n + TILE, :])
        kernel = inner / (norms_ref[:, n : n + TILE] + land_norms - inner)
        cent_ref[:, n : n + TILE] = kernel
        total = total + jnp.sum(kernel, axis=1, keepdims=True)
    mean = total * (1.0 / rows)
    for n in range(0, rows, TILE):
        cent = cent_ref[:, n : n + TILE] - mean
        high = cent.astype(jnp.bfloat16)
        ct_ref[:, n : n + TILE] = high
        low_ref[:, n : n + TILE] = (cent - high.astype(jnp.float32)).astype(jnp.bfloat16)
    mean_ref[:, pl.ds(base, TILE)] = jnp.broadcast_to(mean, (TILE, LANES)).T[:1, :]

    @pl.when(step == 0)
    def _():
        left_ref[:LANES, :] = ct_ref[pl.ds(block, LANES), :]
        left_ref[LANES:, :] = tgs_ref[...]

    both = dot_nt(left_ref[...], ct_ref[...])
    first_ref[:, pl.ds(base, TILE)] = both[:LANES, :]
    cent_ref[:LANES, :TILE] = both[LANES:, :] + dot_nt(left_ref[LANES:, :], low_ref[...])
    rhs_ref[step] = cent_ref[:LANES, pl.ds(block, LANES)].T

    @pl.when(step == pl.num_programs(0) - 1)
    def _():
        lead = jnp.sum(first_ref[...], axis=0, keepdims=True)
        lead_ref[...] = lead
        lead_own = lead_ref[:, pl.ds(block, LANES)]
        mass = jnp.sum(lead_own, axis=1, keepdims=True)
        size = jnp.sum(jnp.abs(lead_own), axis=1, keepdims=True)
        usable = mass > 1e-3 * size
        weight = jnp.where(usable, 1.0 / jnp.where(usable, mass, 1.0), 0.0)
        mine = spread(lead_own) * weight
        for j in range(lead.shape[1] // LANES):
            cols = slice(j * LANES, (j + 1) * LANES)
            part = lead[:, cols]
            column_ref[cols, :] = spread(part) * weight
            rest = first_ref[:, cols] - mine * part
            if j < TILE // LANES:
                message_ref[:LANES, cols] = rest
            else:
                rest_ref[:, slice(cols.start - TILE, cols.stop - TILE)] = rest
        message_ref[LANES:, :] = jnp.zeros((message_ref.shape[0] - LANES, TILE), jnp.float32)
        for j in range(lead.shape[1] // TILE):
            cols = slice(j * TILE, (j + 1) * TILE)
            message_ref[LANES + j : LANES + j + 1, :] = mean_ref[:, cols]
            message_ref[LANES + 8 + j : LANES + 9 + j, :] = lead[:, cols]
        at = LANES + 16
        message_ref[at : at + 1, :LANES] = jnp.broadcast_to(weight, (1, LANES))
        sums = jnp.sum(tgs_ref[...].astype(jnp.float32), axis=1, keepdims=True)
        message_ref[at : at + 1, LANES:] = jnp.broadcast_to(sums, (LANES, LANES)).T[:1, :]


STATS = 24


def stage(core, landmark_fps, fps, norms, tgs):
    rows, length = fps.shape
    landmarks = landmark_fps.shape[0]
    steps = landmarks // TILE
    f32, bf16 = jnp.float32, jnp.bfloat16

    def whole(shape):
        return pl.BlockSpec(shape, lambda i, c: (0,) * len(shape))

    outs = [
        ((steps, LANES, LANES), f32),
        ((LANES, landmarks - TILE), f32),
        ((LANES + STATS, TILE), f32),
        ((1, landmarks), f32),
        ((landmarks, LANES), f32),
    ]
    return pl.pallas_call(
        stage_body,
        grid_spec=pltpu.PrefetchScalarGridSpec(
            num_scalar_prefetch=1,
            grid=(steps,),
            in_specs=[
                pl.BlockSpec((TILE, length), lambda i, c: (i, 0)),
                whole(fps.shape),
                whole(norms.shape),
                whole(tgs.shape),
            ],
            out_specs=[pl.BlockSpec((TILE, rows), lambda i, c: (i, 0))]
            + [whole(s) for s, _ in outs],
            scratch_shapes=[
                pltpu.VMEM((TILE, rows), f32),
                pltpu.VMEM((LANES, landmarks), f32),
                pltpu.VMEM((2 * LANES, rows), bf16),
                pltpu.VMEM((TILE, rows), bf16),
                pltpu.VMEM((1, landmarks), f32),
            ],
        ),
        out_shape=[jax.ShapeDtypeStruct((landmarks, rows), bf16)]
        + [jax.ShapeDtypeStruct(s, d) for s, d in outs],
        compiler_params=pltpu.CompilerParams(vmem_limit_bytes=28 * MIB),
        name="stage",
    )(core, landmark_fps, fps, norms, tgs)


def pieces_body(at_ref, ct_ref, lead_ref, column_ref, rhs_ref, mine_ref, theirs_ref, left_ref):
    count = left_ref.shape[0] // LANES
    for p in range(count):
        at = pl.multiple_of(at_ref[p], LANES)
        left_ref[p * LANES : (p + 1) * LANES, :] = ct_ref[pl.ds(at, LANES), :]

    def store(p, cols, value):
        out = (mine_ref, theirs_ref)[p % 2]
        out[p // 2 * LANES : (p // 2 + 1) * LANES, cols] = value.astype(out.dtype)

    for t in range(1, ct_ref.shape[0] // TILE):
        for q in range(0, count, 2):
            got = dot_nt(
                left_ref[q * LANES : (q + 2) * LANES, :], ct_ref[t * TILE : (t + 1) * TILE, :]
            )
            for p in (q, q + 1):
                at = pl.multiple_of(at_ref[p], LANES)
                column = column_ref[pl.ds(at, LANES), :]
                for h in range(TILE // LANES):
                    lo = t * TILE + h * LANES
                    part = got[(p - q) * LANES : (p - q + 1) * LANES, h * LANES : (h + 1) * LANES]
                    part = part - column * lead_ref[:, lo : lo + LANES]
                    store(p, slice(lo - TILE, lo - TILE + LANES), part)
    for p in range(count):
        lo = ct_ref.shape[0] - TILE
        store(p, slice(lo, lo + LANES), rhs_ref[at_ref[p] // TILE])


def pieces(starts, ct, lead, column, rhs_part):
    shape = (len(starts) // 2 * LANES, ct.shape[0] - TILE + LANES)
    return pl.pallas_call(
        pieces_body,
        in_specs=[pl.BlockSpec(memory_space=pltpu.SMEM)] + vmem(4),
        out_specs=vmem(2),
        out_shape=[
            jax.ShapeDtypeStruct(shape, jnp.float32),
            jax.ShapeDtypeStruct(shape, jnp.bfloat16),
        ],
        scratch_shapes=[pltpu.VMEM((2 * shape[0], ct.shape[1]), jnp.bfloat16)],
        compiler_params=pltpu.CompilerParams(vmem_limit_bytes=28 * MIB),
        name="pieces",
    )(jnp.stack(starts).astype(jnp.int32), ct, lead, column, rhs_part)


CHOL = 32


def exact_dot(a, b, dims=((1,), (0,))):
    return lax.dot_general(
        a, b, (dims, ((), ())), precision=lax.Precision.HIGHEST, preferred_element_type=jnp.float32
    )


def factor_body(blocks, state_ref, out_ref):
    size = state_ref.shape[0]
    out_ref[...] = state_ref[...]
    sub = lax.broadcasted_iota(jnp.int32, (CHOL, LANES), 0)
    lane = lax.broadcasted_iota(jnp.int32, (CHOL, LANES), 1)
    for b in blocks:
        lo, hi = b * CHOL, (b + 1) * CHOL
        diag = out_ref[lo:hi, lo:hi]
        work = jnp.concatenate(
            [
                diag,
                (sub == lane)[:, :CHOL].astype(jnp.float32),
                jnp.zeros((CHOL, LANES - 2 * CHOL), jnp.float32),
            ],
            axis=1,
        )

        for k in range(CHOL):
            col = jnp.broadcast_to(work[:, k : k + 1], work.shape)
            row = work[k : k + 1, :] / col[k : k + 1, :]
            work = work - jnp.where(sub > k, col, 0.0) * row
        pivots = jnp.sum(jnp.where(sub == lane, work, 0.0), axis=1, keepdims=True)
        inverse = work[:, CHOL : 2 * CHOL] / jnp.sqrt(pivots)
        done = exact_dot(inverse, out_ref[lo:hi, :])
        out_ref[lo:hi, :] = done
        if hi < size:
            left = hi // LANES * LANES
            cols = slice(left, size + -(-hi // LANES) * LANES)
            out_ref[hi:, cols] = out_ref[hi:, cols] - exact_dot(
                done[:, hi:size], done[:, cols], ((0,), (0,))
            )


def eliminate_blocks(state, blocks):
    return pl.pallas_call(
        functools.partial(factor_body, blocks),
        in_specs=vmem(1),
        out_specs=vmem(1)[0],
        out_shape=jax.ShapeDtypeStruct(state.shape, jnp.float32),
        compiler_params=pltpu.CompilerParams(vmem_limit_bytes=28 * MIB),
        name="factor",
    )(state)


def pack_body(at_ref, index_ref, fps_ref, packed_ref, slots_ref, key_ref, pick_ref):
    rows, landmarks = fps_ref.shape[0], index_ref.shape[1]
    capacity = packed_ref.shape[0]
    f32 = jnp.float32
    index = index_ref[...].astype(f32)
    owner = jnp.floor(index * (1.0 / rows))
    key_ref[1:2, :] = index - owner * rows
    device = lax.broadcasted_iota(jnp.int32, (16, TILE), 0).astype(f32)
    before = lax.broadcasted_iota(jnp.int32, (TILE, TILE), 0)
    before = (before < lax.broadcasted_iota(jnp.int32, (TILE, TILE), 1)).astype(jnp.bfloat16)
    owners = [owner[:, n : n + TILE] for n in range(0, landmarks, TILE)]
    owned = [(device == o).astype(f32) for o in owners]
    within = dot_nn(jnp.concatenate(owned, axis=0).astype(jnp.bfloat16), before)
    ahead = jnp.zeros((16, 1), f32)
    slot_in = lax.broadcasted_iota(jnp.int32, (capacity, TILE), 0).astype(f32)
    for b, o in enumerate(owners):
        counts = within[b * 16 : (b + 1) * 16, :] + ahead
        rank = jnp.sum(owned[b] * counts, axis=0, keepdims=True)
        ahead = ahead + jnp.sum(owned[b], axis=1, keepdims=True)
        slot = o * capacity + rank
        for h in range(0, TILE, LANES):
            lo = b * TILE + h
            slots_ref[lo : lo + LANES, :] = spread(slot[:, h : h + LANES])
        key = jnp.where(o == at_ref[0].astype(f32), rank, -1.0)
        pick_ref[:, b * TILE : (b + 1) * TILE] = (slot_in == key).astype(jnp.bfloat16)
    packed = jnp.zeros(packed_ref.shape, f32)
    for r in range(0, rows, TILE):
        row_in = lax.broadcasted_iota(jnp.int32, (TILE, landmarks), 0).astype(f32) + r
        here = (row_in == key_ref[1:2, :]).astype(jnp.bfloat16)
        chosen = dot_nt(pick_ref[...], here).astype(jnp.bfloat16)
        packed = packed + dot_nn(chosen, fps_ref[r : r + TILE, :])
    packed_ref[...] = packed.astype(jnp.bfloat16)


def pack(position, landmark_index, fingerprints):
    landmarks = landmark_index.shape[0]
    capacity = landmarks // 8
    return pl.pallas_call(
        pack_body,
        in_specs=[pl.BlockSpec(memory_space=pltpu.SMEM)] + vmem(2),
        out_specs=vmem(2),
        out_shape=[
            jax.ShapeDtypeStruct((capacity, fingerprints.shape[1]), jnp.bfloat16),
            jax.ShapeDtypeStruct((landmarks, LANES), jnp.float32),
        ],
        scratch_shapes=[
            pltpu.VMEM((8, landmarks), jnp.float32),
            pltpu.VMEM((capacity, landmarks), jnp.bfloat16),
        ],
        compiler_params=pltpu.CompilerParams(vmem_limit_bytes=28 * MIB),
        name="pack",
    )(jnp.reshape(position, (1,)), landmark_index[None, :], fingerprints)


def place_body(count, base_ref, slots_ref, *refs):
    chunks, before, out_ref = refs[:count], refs[count:-1], refs[-1]
    slots = slots_ref[...]
    lane = lax.broadcasted_iota(jnp.int32, slots.shape, 1).astype(jnp.float32)
    got = before[0][...].astype(jnp.float32) if before else jnp.zeros(out_ref.shape, jnp.float32)
    for n, chunk in enumerate(chunks):
        inside = slots - base_ref[n].astype(jnp.float32)
        chosen = jnp.concatenate(
            [
                (inside == lane + h).astype(jnp.float32)
                for h in range(0, chunk.shape[0], LANES)
            ],
            axis=1,
        )
        got = got + dot_nn(chosen.astype(jnp.bfloat16), chunk[...])
    out_ref[...] = got.astype(jnp.bfloat16)


def place(owners, chunks, slots, before=None):
    capacity, length = chunks[0].shape
    landmarks = slots.shape[0]
    tile = pl.BlockSpec((TILE, length), lambda i: (i, 0))
    extra = [] if before is None else [before]
    return pl.pallas_call(
        functools.partial(place_body, len(chunks)),
        grid=(landmarks // TILE,),
        in_specs=[
            pl.BlockSpec(memory_space=pltpu.SMEM),
            pl.BlockSpec((TILE, LANES), lambda i: (i, 0)),
        ]
        + [pl.BlockSpec((capacity, length), lambda i: (0, 0))] * len(chunks)
        + [tile] * len(extra),
        out_specs=tile,
        out_shape=jax.ShapeDtypeStruct((landmarks, length), jnp.bfloat16),
        compiler_params=pltpu.CompilerParams(vmem_limit_bytes=28 * MIB),
        name="place",
    )((jnp.stack(owners) * capacity).astype(jnp.int32), slots, *chunks, *extra)


def landmarks_everywhere(fingerprints, landmark_index):
    position = lax.axis_index("dp")
    packed, slots = pack(position, landmark_index, fingerprints)
    held = {0: packed}
    for perm, mask in ((FAR, 8), (NEAR, 4), (ROW, 2)):
        held[mask] = send(packed, perm)
    held[12] = send(held[8], NEAR)
    held[6] = send(held[4], ROW)
    held[10] = send(held[8], ROW)
    held[14] = send(held[12], ROW)
    result = None
    for masks in ((0, 2, 4, 8), (6, 12, 10, 14)):
        owners, chunks = [], []
        for m in masks:
            chunk = held[m]
            if m in (6, 10, 14):
                chunk = after(chunk, result)
            owners += [position ^ m, position ^ m ^ 1]
            chunks += [chunk, send(chunk, CORE)]
        result = place(owners, chunks, slots, result)
    return result


def local_16(fingerprints, targets, landmark_index):
    rows_dev = fingerprints.shape[0]
    total_rows = rows_dev * 16
    landmarks = landmark_index.shape[0]
    share = landmarks // 16
    width = PB
    position = lax.axis_index("dp")
    core = position % 2
    row = (position // 2) % 2
    layer = position // 4
    scale = 1.0 / (ridge_weight * total_rows)

    fps = jnp.concatenate([fingerprints, send(fingerprints, CORE)], axis=0)
    tgs = jnp.concatenate([targets, send(targets, CORE)], axis=0)
    chip_rows = 2 * rows_dev
    landmark_fps = landmarks_everywhere(fingerprints, landmark_index)
    norms = sq_norms(landmark_fps)
    ct, rhs_part, rest_rows, message, lead, column = stage(
        jnp.reshape(core, (1,)), landmark_fps, fps, sq_norms(fps)[None, :], tgs.T
    )
    panel_cols, other_cols = slice(0, width), slice(width, landmarks)
    f32, bf16 = jnp.float32, jnp.bfloat16

    def gram_rows(masks, ct):
        starts = []
        for m in masks:
            there = ((layer ^ m) * 4 + core) * share
            starts += [there + row * 2 * share, there + (1 - row) * 2 * share]
        return pieces(starts, ct, lead, column, rhs_part)

    def merge(x, y):
        return jnp.concatenate([x[:share] + y[:share], x[share:], y[share:]], axis=0)

    planes = [[2 * j + c for j in range(8)] for c in range(2)]
    part = lax.psum(rest_rows, "dp", axis_index_groups=planes)
    message_row = send(message, ROW)
    mine_32, theirs_32 = gram_rows((3, 2), ct)
    other_32 = send(theirs_32, ROW)
    message = merge(message, after(message_row, mine_32))
    message_near = send(message, NEAR)
    mine_10, theirs_10 = gram_rows((1, 0), after(ct, message))
    other_10 = send(theirs_10, ROW)
    message = merge(message, after(message_near, mine_10))
    message_far = send(message, FAR)
    sums_32 = mine_32 + after(other_32, message).astype(f32)
    three = sums_32[:share].astype(bf16)
    other_two = send(three, NEAR)
    message = merge(message, after(message_far, three))

    stats = message[share:].reshape(8, STATS, TILE)
    means = stats[:, :8].reshape(8, landmarks)
    leads = stats[:, 8:16].reshape(8, landmarks)
    lead_weights, target_sums = stats[:, 16, :1], stats[:, 16, LANES:]
    shift = means - jnp.mean(means, axis=0, keepdims=True)
    left_terms = jnp.concatenate([shift * chip_rows, leads], axis=0)
    right_terms = jnp.concatenate([shift, leads * lead_weights], axis=0)

    def system_part(sums, start, cols):
        rows_fps = lax.dynamic_slice_in_dim(landmark_fps, start, share, 0)
        terms = lax.dynamic_slice_in_dim(left_terms, start, share, 1)
        return (sums + highest(terms, right_terms[:, cols])) * scale + tanimoto(
            rows_fps, landmark_fps[cols], norms[cols]
        )

    def in_order(x, other, high):
        size = x.shape[0]
        return lax.dynamic_slice_in_dim(
            jnp.concatenate([x, other, x], axis=0), high * size, 2 * size, 0
        )

    def both_blocks(block):
        return in_order(block, send(block, CORE), core)

    corner = both_blocks(system_part(message[:share], core * share, panel_cols))
    state = jnp.concatenate([corner, jnp.eye(width, dtype=f32)], axis=1)

    calls = [(b, b + 1) for b in range(0, width // CHOL, 2)]
    state = eliminate_blocks(state, calls[0])
    two = (sums_32[share:] + after(other_two, state).astype(f32)).astype(bf16)
    got_two = send(two, FAR)
    state = eliminate_blocks(after(state, two), calls[1])
    sums_10 = mine_10 + after(other_10, state).astype(f32)
    one = sums_10[:share].astype(bf16)
    got_one = send(one, NEAR)
    state = eliminate_blocks(after(state, one), calls[2])
    state = eliminate_blocks(state, calls[3])
    block = both_blocks(system_part(after(part, state), core * share, other_cols))
    panel_rows = jnp.concatenate([corner, block], axis=1)
    factor = exact_dot(state[:, width:], panel_rows)

    own = sums_10[share:] + got_one.astype(f32) + got_two.astype(f32)
    start = position * share
    rest = system_part(own[:, : landmarks - width], start, other_cols)
    own_shift = lax.dynamic_slice_in_dim(shift, start, share, 1)
    rhs = (own[:, landmarks - width :] + highest(own_shift, target_sums)) / math.sqrt(
        ridge_weight * total_rows
    )
    own_panel = lax.dynamic_slice_in_dim(panel_rows, start, share, 1)
    own_factor = lax.dynamic_slice_in_dim(factor, start, share, 1)
    system_rows = jnp.concatenate([own_panel.T, rest], axis=1)
    trailing = system_rows - highest(own_factor, factor)
    return (rhs, own_factor.T, trailing)


def solution(mesh):
    local = local_16 if mesh.shape["dp"] == 16 else local_any
    in_specs = (P(("groups", "dp"), None), P(("groups", "dp"), None), P("groups"))
    out_specs = (P(("groups", "dp"), None), P(("groups", "dp"), None), P(("groups", "dp"), None))
    return jax.shard_map(local, mesh=mesh, in_specs=in_specs, out_specs=out_specs, check_vma=False)
```

```python
import functools
import math

import jax
import jax.numpy as jnp
from jax import lax
from jax.experimental import pallas as pl
from jax.experimental.pallas import tpu as pltpu
from jax.sharding import PartitionSpec as P

PB = 256


ridge_weight = 0.01


def sq_norms(row_block):
    wide_rows = row_block.astype(jnp.float32)
    return jnp.sum(wide_rows * wide_rows, axis=1)


def tanimoto(row_block, landmark_fps, landmark_norms):
    inner_prod = lax.dot_general(
        row_block, landmark_fps, (((1,), (1,)), ((), ())), preferred_element_type=jnp.float32
    )
    row_norms = sq_norms(row_block)
    return inner_prod / (row_norms[:, None] + landmark_norms[None, :] - inner_prod)


def local_any(fingerprints, targets, landmark_index):
    rows_dev = fingerprints.shape[0]
    devices = lax.axis_size("dp")
    total_rows = rows_dev * devices
    landmarks = landmark_index.shape[0]
    land_share = landmarks // devices
    position = lax.axis_index("dp")
    owner_dev = landmark_index // rows_dev
    offset = landmark_index % rows_dev
    is_mine = owner_dev == position
    capacity = 2 * land_share
    owner_onehot = (owner_dev[:, None] == jnp.arange(devices, dtype=jnp.int32)[None, :]).astype(
        jnp.int32
    )
    owner_rank = jnp.sum(jnp.cumsum(owner_onehot, axis=0) * owner_onehot, axis=1) - 1
    slot_rows = (
        jnp.zeros((capacity,), jnp.int32)
        .at[jnp.where(is_mine, owner_rank, capacity)]
        .set(offset, mode="drop")
    )
    packed = fingerprints[slot_rows]
    gathered = lax.all_gather(packed, "dp", axis=0, tiled=True)
    landmark_fps = gathered[owner_dev * capacity + owner_rank]
    landmark_norms = sq_norms(landmark_fps)
    kernel = tanimoto(fingerprints, landmark_fps, landmark_norms)
    col_total = lax.psum(jnp.sum(kernel, axis=0), "dp")
    col_mean = col_total / total_rows
    centred = (kernel - col_mean[None, :]).astype(jnp.bfloat16)
    joined = jnp.concatenate([centred, targets], axis=1)
    totals = lax.psum_scatter(
        lax.dot_general(
            centred, joined, (((0,), (0,)), ((), ())), preferred_element_type=jnp.float32
        ),
        "dp",
        scatter_dimension=0,
        tiled=True,
    )
    gram_rows = totals[:, :landmarks]
    rhs_rows = totals[:, landmarks:]
    rhs = rhs_rows / math.sqrt(ridge_weight * total_rows)
    own_fps = lax.dynamic_slice_in_dim(landmark_fps, position * land_share, land_share, 0)
    system_rows = gram_rows / (ridge_weight * total_rows) + tanimoto(
        own_fps, landmark_fps, landmark_norms
    )
    panel_width = PB
    column_block = lax.all_gather(system_rows[:, :panel_width], "dp", axis=0, tiled=True)
    corner = jnp.linalg.cholesky(column_block[:panel_width])
    panel_full = lax.linalg.triangular_solve(
        corner, column_block, left_side=False, lower=True, transpose_a=True
    )
    panel_own = lax.dynamic_slice_in_dim(panel_full, position * land_share, land_share, 0)
    trailing = system_rows - jnp.dot(panel_own, panel_full.T, precision=lax.Precision.HIGHEST)
    return (rhs, panel_own, trailing)


CORE = [(i, i ^ 1) for i in range(16)]
ROW = [(i, i ^ 2) for i in range(16)]
NEAR = [(i, i ^ 4) for i in range(16)]
FAR = [(i, i ^ 8) for i in range(16)]
LANES = 128
TILE = 256
MIB = 2**20
LITTLE = pl.CostEstimate(flops=1, transcendentals=0, bytes_accessed=1)


def send(x, perm):
    return lax.ppermute(x, "dp", perm)


def highest(a, b):
    return lax.dot_general(
        a,
        b,
        (((0,), (0,)), ((), ())),
        precision=lax.Precision.HIGHEST,
        preferred_element_type=jnp.float32,
    )


def dot_nt(a, b):
    return lax.dot_general(a, b, (((1,), (1,)), ((), ())), preferred_element_type=jnp.float32)


def dot_nn(a, b):
    return lax.dot_general(a, b, (((1,), (0,)), ((), ())), preferred_element_type=jnp.float32)


def after(x, *earlier):
    return lax.optimization_barrier((x,) + earlier)[0]


def vmem(count):
    return [pl.BlockSpec(memory_space=pltpu.VMEM)] * count


def spread(row_vector):
    return jnp.broadcast_to(row_vector, (LANES, LANES)).T


def stage_body(
    core_ref, land_ref, fps_ref, norms_ref, tgs_ref,
    ct_ref, rhs_ref, rest_ref, message_ref, lead_ref, column_ref,
    cent_ref, first_ref, left_ref, mean_ref,
):
    step = pl.program_id(0)
    rows = fps_ref.shape[0]
    base = pl.multiple_of(step * TILE, TILE)
    block = pl.multiple_of(core_ref[0] * LANES, LANES)
    tile = land_ref[...]
    wide = tile.astype(jnp.float32)
    land_norms = jnp.sum(wide * wide, axis=1, keepdims=True)
    total = jnp.zeros((TILE, 1), jnp.float32)
    for n in range(0, rows, TILE):
        inner = dot_nt(tile, fps_ref[n : n + TILE, :])
        kernel = inner / (norms_ref[:, n : n + TILE] + land_norms - inner)
        cent_ref[:, n : n + TILE] = kernel
        total = total + jnp.sum(kernel, axis=1, keepdims=True)
    mean = total * (1.0 / rows)
    for n in range(0, rows, TILE):
        cent = cent_ref[:, n : n + TILE] - mean
        cent_ref[:, n : n + TILE] = cent
        ct_ref[:, n : n + TILE] = cent.astype(jnp.bfloat16)
    own = cent_ref[pl.ds(block, LANES), :]
    low = (own - ct_ref[pl.ds(block, LANES), :].astype(jnp.float32)).astype(jnp.bfloat16)
    mean_ref[:, pl.ds(base, TILE)] = jnp.broadcast_to(mean, (TILE, LANES)).T[:1, :]

    @pl.when(step == 0)
    def _():
        left_ref[:LANES, :] = ct_ref[pl.ds(block, LANES), :]
        left_ref[LANES:, :] = tgs_ref[...]

    both = dot_nt(left_ref[...], ct_ref[...])
    first_ref[:, pl.ds(base, TILE)] = both[:LANES, :]
    cent_ref[:LANES, :TILE] = both[LANES:, :]
    high_part = cent_ref[:LANES, pl.ds(block, LANES)]
    rhs_ref[step] = (high_part + dot_nt(left_ref[LANES:, :], low)).T

    @pl.when(step == pl.num_programs(0) - 1)
    def _():
        lead = jnp.sum(first_ref[...], axis=0, keepdims=True)
        lead_ref[...] = lead
        lead_own = lead_ref[:, pl.ds(block, LANES)]
        mass = jnp.sum(lead_own, axis=1, keepdims=True)
        size = jnp.sum(jnp.abs(lead_own), axis=1, keepdims=True)
        usable = mass > 1e-3 * size
        weight = jnp.where(usable, 1.0 / jnp.where(usable, mass, 1.0), 0.0)
        mine = spread(lead_own) * weight
        for j in range(lead.shape[1] // LANES):
            cols = slice(j * LANES, (j + 1) * LANES)
            part = lead[:, cols]
            column_ref[cols, :] = spread(part) * weight
            rest = first_ref[:, cols] - mine * part
            if j < TILE // LANES:
                message_ref[:LANES, cols] = rest
            else:
                rest_ref[:, slice(cols.start - TILE, cols.stop - TILE)] = rest
        message_ref[LANES:, :] = jnp.zeros((message_ref.shape[0] - LANES, TILE), jnp.float32)
        for j in range(lead.shape[1] // TILE):
            cols = slice(j * TILE, (j + 1) * TILE)
            message_ref[LANES + j : LANES + j + 1, :] = mean_ref[:, cols]
            message_ref[LANES + 8 + j : LANES + 9 + j, :] = lead[:, cols]
        at = LANES + 16
        message_ref[at : at + 1, :LANES] = jnp.broadcast_to(weight, (1, LANES))
        sums = jnp.sum(tgs_ref[...].astype(jnp.float32), axis=1, keepdims=True)
        message_ref[at : at + 1, LANES:] = jnp.broadcast_to(sums, (LANES, LANES)).T[:1, :]


STATS = 24


def stage(core, landmark_fps, fps, norms, tgs):
    rows, length = fps.shape
    landmarks = landmark_fps.shape[0]
    steps = landmarks // TILE
    f32, bf16 = jnp.float32, jnp.bfloat16

    def whole(shape):
        return pl.BlockSpec(shape, lambda i, c: (0,) * len(shape))

    outs = [
        ((steps, LANES, LANES), f32),
        ((LANES, landmarks - TILE), f32),
        ((LANES + STATS, TILE), f32),
        ((1, landmarks), f32),
        ((landmarks, LANES), f32),
    ]
    return pl.pallas_call(
        stage_body,
        grid_spec=pltpu.PrefetchScalarGridSpec(
            num_scalar_prefetch=1,
            grid=(steps,),
            in_specs=[
                pl.BlockSpec((TILE, length), lambda i, c: (i, 0)),
                whole(fps.shape),
                whole(norms.shape),
                whole(tgs.shape),
            ],
            out_specs=[pl.BlockSpec((TILE, rows), lambda i, c: (i, 0))]
            + [whole(s) for s, _ in outs],
            scratch_shapes=[
                pltpu.VMEM((TILE, rows), f32),
                pltpu.VMEM((LANES, landmarks), f32),
                pltpu.VMEM((2 * LANES, rows), bf16),
                pltpu.VMEM((1, landmarks), f32),
            ],
        ),
        out_shape=[jax.ShapeDtypeStruct((landmarks, rows), bf16)]
        + [jax.ShapeDtypeStruct(s, d) for s, d in outs],
        compiler_params=pltpu.CompilerParams(vmem_limit_bytes=28 * MIB),
        name="stage",
    )(core, landmark_fps, fps, norms, tgs)


def pieces_body(at_ref, ct_ref, lead_ref, column_ref, rhs_ref, mine_ref, theirs_ref, left_ref):
    count = left_ref.shape[0] // LANES
    for p in range(count):
        at = pl.multiple_of(at_ref[p], LANES)
        left_ref[p * LANES : (p + 1) * LANES, :] = ct_ref[pl.ds(at, LANES), :]

    def store(p, cols, value):
        out = (mine_ref, theirs_ref)[p % 2]
        out[p // 2 * LANES : (p // 2 + 1) * LANES, cols] = value.astype(out.dtype)

    for t in range(1, ct_ref.shape[0] // TILE):
        for q in range(0, count, 2):
            got = dot_nt(
                left_ref[q * LANES : (q + 2) * LANES, :], ct_ref[t * TILE : (t + 1) * TILE, :]
            )
            for p in (q, q + 1):
                at = pl.multiple_of(at_ref[p], LANES)
                column = column_ref[pl.ds(at, LANES), :]
                for h in range(TILE // LANES):
                    lo = t * TILE + h * LANES
                    part = got[(p - q) * LANES : (p - q + 1) * LANES, h * LANES : (h + 1) * LANES]
                    part = part - column * lead_ref[:, lo : lo + LANES]
                    store(p, slice(lo - TILE, lo - TILE + LANES), part)
    for p in range(count):
        lo = ct_ref.shape[0] - TILE
        store(p, slice(lo, lo + LANES), rhs_ref[at_ref[p] // TILE])


def pieces(starts, ct, lead, column, rhs_part):
    shape = (len(starts) // 2 * LANES, ct.shape[0] - TILE + LANES)
    return pl.pallas_call(
        pieces_body,
        in_specs=[pl.BlockSpec(memory_space=pltpu.SMEM)] + vmem(4),
        out_specs=vmem(2),
        out_shape=[
            jax.ShapeDtypeStruct(shape, jnp.float32),
            jax.ShapeDtypeStruct(shape, jnp.bfloat16),
        ],
        scratch_shapes=[pltpu.VMEM((2 * shape[0], ct.shape[1]), jnp.bfloat16)],
        compiler_params=pltpu.CompilerParams(vmem_limit_bytes=28 * MIB),
        cost_estimate=LITTLE,
        name="pieces",
    )(jnp.stack(starts).astype(jnp.int32), ct, lead, column, rhs_part)


CHOL = 32


def exact_dot(a, b, dims=((1,), (0,))):
    return lax.dot_general(
        a, b, (dims, ((), ())), precision=lax.Precision.HIGHEST, preferred_element_type=jnp.float32
    )


def factor_body(blocks, state_ref, out_ref):
    size = state_ref.shape[0]
    out_ref[...] = state_ref[...]
    sub = lax.broadcasted_iota(jnp.int32, (CHOL, LANES), 0)
    lane = lax.broadcasted_iota(jnp.int32, (CHOL, LANES), 1)
    for b in blocks:
        lo, hi = b * CHOL, (b + 1) * CHOL
        diag = out_ref[lo:hi, lo:hi]
        work = jnp.concatenate(
            [
                diag,
                (sub == lane)[:, :CHOL].astype(jnp.float32),
                jnp.zeros((CHOL, LANES - 2 * CHOL), jnp.float32),
            ],
            axis=1,
        )

        for k in range(CHOL):
            col = jnp.broadcast_to(work[:, k : k + 1], work.shape)
            row = work[k : k + 1, :] / col[k : k + 1, :]
            work = work - jnp.where(sub > k, col, 0.0) * row
        pivots = jnp.sum(jnp.where(sub == lane, work, 0.0), axis=1, keepdims=True)
        inverse = work[:, CHOL : 2 * CHOL] / jnp.sqrt(pivots)
        done = exact_dot(inverse, out_ref[lo:hi, :])
        out_ref[lo:hi, :] = done
        if hi < size:
            left = hi // LANES * LANES
            cols = slice(left, size + -(-hi // LANES) * LANES)
            out_ref[hi:, cols] = out_ref[hi:, cols] - exact_dot(
                done[:, hi:size], done[:, cols], ((0,), (0,))
            )


def eliminate_blocks(state, blocks):
    return pl.pallas_call(
        functools.partial(factor_body, blocks),
        in_specs=vmem(1),
        out_specs=vmem(1)[0],
        out_shape=jax.ShapeDtypeStruct(state.shape, jnp.float32),
        compiler_params=pltpu.CompilerParams(vmem_limit_bytes=28 * MIB),
        cost_estimate=LITTLE,
        name="factor",
    )(state)


def finish_body(
    scale, at_ref, state_ref, corner_ref, sums_ref, added_ref, rest_ref,
    panel_ref, trailing_ref, factor_ref, own_ref,
):
    width = corner_ref.shape[0]
    start = pl.multiple_of(at_ref[0], LANES)
    inverse = state_ref[:, width:]
    own_ref[:, :width] = corner_ref[...]
    factor_ref[:, :width] = exact_dot(inverse, corner_ref[...])
    for lo in range(0, rest_ref.shape[1], TILE):
        cols = slice(lo, lo + TILE)
        rows = sums_ref[:, cols].astype(jnp.float32) * scale + added_ref[:, cols]
        own_ref[:, lo + width : lo + width + TILE] = rows
        factor_ref[:, lo + width : lo + width + TILE] = exact_dot(inverse, rows)
    panel = factor_ref[:, pl.ds(start, LANES)].T
    panel_ref[...] = panel
    first = own_ref[:, pl.ds(start, LANES)].T
    trailing_ref[:, :width] = first - exact_dot(panel, factor_ref[:, :width])
    for lo in range(0, rest_ref.shape[1], TILE):
        here = slice(lo + width, lo + width + TILE)
        trailing_ref[:, here] = rest_ref[:, lo : lo + TILE] - exact_dot(panel, factor_ref[:, here])


def finish(scale, start, state, corner, sums, added, rest):
    width, landmarks = corner.shape[0], rest.shape[1] + corner.shape[0]
    f32 = jnp.float32
    return pl.pallas_call(
        functools.partial(finish_body, scale),
        in_specs=[pl.BlockSpec(memory_space=pltpu.SMEM)] + vmem(5),
        out_specs=vmem(2),
        out_shape=[
            jax.ShapeDtypeStruct((LANES, width), f32),
            jax.ShapeDtypeStruct((LANES, landmarks), f32),
        ],
        scratch_shapes=[pltpu.VMEM((width, landmarks), f32), pltpu.VMEM((width, landmarks), f32)],
        compiler_params=pltpu.CompilerParams(vmem_limit_bytes=28 * MIB),
        name="finish",
    )(jnp.reshape(start, (1,)), state, corner, sums, added, rest)


def pack_body(at_ref, index_ref, fps_ref, packed_ref, slots_ref, key_ref, pick_ref):
    rows, landmarks = fps_ref.shape[0], index_ref.shape[1]
    capacity = packed_ref.shape[0]
    f32 = jnp.float32
    index = index_ref[...].astype(f32)
    owner = jnp.floor(index * (1.0 / rows))
    key_ref[1:2, :] = index - owner * rows
    device = lax.broadcasted_iota(jnp.int32, (16, TILE), 0).astype(f32)
    before = lax.broadcasted_iota(jnp.int32, (TILE, TILE), 0)
    before = (before < lax.broadcasted_iota(jnp.int32, (TILE, TILE), 1)).astype(jnp.bfloat16)
    owners = [owner[:, n : n + TILE] for n in range(0, landmarks, TILE)]
    owned = [(device == o).astype(f32) for o in owners]
    within = dot_nn(jnp.concatenate(owned, axis=0).astype(jnp.bfloat16), before)
    ahead = jnp.zeros((16, 1), f32)
    slot_in = lax.broadcasted_iota(jnp.int32, (capacity, TILE), 0).astype(f32)
    for b, o in enumerate(owners):
        counts = within[b * 16 : (b + 1) * 16, :] + ahead
        rank = jnp.sum(owned[b] * counts, axis=0, keepdims=True)
        ahead = ahead + jnp.sum(owned[b], axis=1, keepdims=True)
        slot = o * capacity + rank
        for h in range(0, TILE, LANES):
            lo = b * TILE + h
            slots_ref[lo : lo + LANES, :] = spread(slot[:, h : h + LANES])
        key = jnp.where(o == at_ref[0].astype(f32), rank, -1.0)
        pick_ref[:, b * TILE : (b + 1) * TILE] = (slot_in == key).astype(jnp.bfloat16)
    packed = jnp.zeros(packed_ref.shape, f32)
    for r in range(0, rows, TILE):
        row_in = lax.broadcasted_iota(jnp.int32, (TILE, landmarks), 0).astype(f32) + r
        here = (row_in == key_ref[1:2, :]).astype(jnp.bfloat16)
        chosen = dot_nt(pick_ref[...], here).astype(jnp.bfloat16)
        packed = packed + dot_nn(chosen, fps_ref[r : r + TILE, :])
    packed_ref[...] = packed.astype(jnp.bfloat16)


def pack(position, landmark_index, fingerprints):
    landmarks = landmark_index.shape[0]
    capacity = landmarks // 8
    return pl.pallas_call(
        pack_body,
        in_specs=[pl.BlockSpec(memory_space=pltpu.SMEM)] + vmem(2),
        out_specs=vmem(2),
        out_shape=[
            jax.ShapeDtypeStruct((capacity, fingerprints.shape[1]), jnp.bfloat16),
            jax.ShapeDtypeStruct((landmarks, LANES), jnp.float32),
        ],
        scratch_shapes=[
            pltpu.VMEM((8, landmarks), jnp.float32),
            pltpu.VMEM((capacity, landmarks), jnp.bfloat16),
        ],
        compiler_params=pltpu.CompilerParams(vmem_limit_bytes=28 * MIB),
        name="pack",
    )(jnp.reshape(position, (1,)), landmark_index[None, :], fingerprints)


def place_body(count, base_ref, slots_ref, *refs):
    chunks, before, out_ref = refs[:count], refs[count:-1], refs[-1]
    slots = slots_ref[...]
    lane = lax.broadcasted_iota(jnp.int32, slots.shape, 1).astype(jnp.float32)
    got = before[0][...].astype(jnp.float32) if before else jnp.zeros(out_ref.shape, jnp.float32)
    for n, chunk in enumerate(chunks):
        inside = slots - base_ref[n].astype(jnp.float32)
        chosen = jnp.concatenate(
            [
                (inside == lane + h).astype(jnp.float32)
                for h in range(0, chunk.shape[0], LANES)
            ],
            axis=1,
        )
        got = got + dot_nn(chosen.astype(jnp.bfloat16), chunk[...])
    out_ref[...] = got.astype(jnp.bfloat16)


def place(owners, chunks, slots, before=None):
    capacity, length = chunks[0].shape
    landmarks = slots.shape[0]
    tile = pl.BlockSpec((TILE, length), lambda i: (i, 0))
    extra = [] if before is None else [before]
    return pl.pallas_call(
        functools.partial(place_body, len(chunks)),
        grid=(landmarks // TILE,),
        in_specs=[
            pl.BlockSpec(memory_space=pltpu.SMEM),
            pl.BlockSpec((TILE, LANES), lambda i: (i, 0)),
        ]
        + [pl.BlockSpec((capacity, length), lambda i: (0, 0))] * len(chunks)
        + [tile] * len(extra),
        out_specs=tile,
        out_shape=jax.ShapeDtypeStruct((landmarks, length), jnp.bfloat16),
        compiler_params=pltpu.CompilerParams(vmem_limit_bytes=28 * MIB),
        name="place",
    )((jnp.stack(owners) * capacity).astype(jnp.int32), slots, *chunks, *extra)


def landmarks_everywhere(fingerprints, landmark_index):
    position = lax.axis_index("dp")
    packed, slots = pack(position, landmark_index, fingerprints)
    held = {0: packed}
    for perm, mask in ((FAR, 8), (NEAR, 4), (ROW, 2)):
        held[mask] = send(packed, perm)
    held[12] = send(held[8], NEAR)
    held[6] = send(held[4], ROW)
    held[10] = send(held[8], ROW)
    held[14] = send(held[12], ROW)
    result = None
    for masks in ((0, 2, 4, 8), (6, 12, 10, 14)):
        owners, chunks = [], []
        for m in masks:
            chunk = held[m]
            if m in (6, 10, 14):
                chunk = after(chunk, result)
            owners += [position ^ m, position ^ m ^ 1]
            chunks += [chunk, send(chunk, CORE)]
        result = place(owners, chunks, slots, result)
    return result


def local_16(fingerprints, targets, landmark_index):
    rows_dev = fingerprints.shape[0]
    total_rows = rows_dev * 16
    landmarks = landmark_index.shape[0]
    share = landmarks // 16
    width = PB
    position = lax.axis_index("dp")
    core = position % 2
    row = (position // 2) % 2
    layer = position // 4
    scale = 1.0 / (ridge_weight * total_rows)

    fps = jnp.concatenate([fingerprints, send(fingerprints, CORE)], axis=0)
    tgs = jnp.concatenate([targets, send(targets, CORE)], axis=0)
    chip_rows = 2 * rows_dev
    landmark_fps = landmarks_everywhere(fingerprints, landmark_index)
    norms = sq_norms(landmark_fps)
    ct, rhs_part, rest_rows, message, lead, column = stage(
        jnp.reshape(core, (1,)), landmark_fps, fps, sq_norms(fps)[None, :], tgs.T
    )
    panel_cols, other_cols = slice(0, width), slice(width, landmarks)
    f32, bf16 = jnp.float32, jnp.bfloat16

    def gram_rows(masks, ct):
        starts = []
        for m in masks:
            there = ((layer ^ m) * 4 + core) * share
            starts += [there + row * 2 * share, there + (1 - row) * 2 * share]
        return pieces(starts, ct, lead, column, rhs_part)

    def merge(x, y):
        return jnp.concatenate([x[:share] + y[:share], x[share:], y[share:]], axis=0)

    planes = [[2 * j + c for j in range(8)] for c in range(2)]
    part = lax.psum(rest_rows, "dp", axis_index_groups=planes)
    message_row = send(message, ROW)
    mine_32, theirs_32 = gram_rows((3, 2), ct)
    other_32 = send(theirs_32, ROW)
    message = merge(message, after(message_row, mine_32))
    message_near = send(message, NEAR)
    mine_10, theirs_10 = gram_rows((1, 0), after(ct, message))
    other_10 = send(theirs_10, ROW)
    message = merge(message, after(message_near, mine_10))
    message_far = send(message, FAR)
    sums_32 = mine_32 + after(other_32, message).astype(f32)
    three = sums_32[:share].astype(bf16)
    other_two = send(three, NEAR)
    message = merge(message, after(message_far, three))

    stats = message[share:].reshape(8, STATS, TILE)
    means = stats[:, :8].reshape(8, landmarks)
    leads = stats[:, 8:16].reshape(8, landmarks)
    lead_weights, target_sums = stats[:, 16, :1], stats[:, 16, LANES:]
    shift = means - jnp.mean(means, axis=0, keepdims=True)
    left_terms = jnp.concatenate([shift * chip_rows, leads], axis=0)
    right_terms = jnp.concatenate([shift, leads * lead_weights], axis=0)

    def added_part(start, cols):
        rows_fps = lax.dynamic_slice_in_dim(landmark_fps, start, share, 0)
        terms = lax.dynamic_slice_in_dim(left_terms, start, share, 1)
        return highest(terms, right_terms[:, cols]) * scale + tanimoto(
            rows_fps, landmark_fps[cols], norms[cols]
        )

    def in_order(x, other, high):
        size = x.shape[0]
        return lax.dynamic_slice_in_dim(
            jnp.concatenate([x, other, x], axis=0), high * size, 2 * size, 0
        )

    def both_blocks(block):
        return in_order(block, send(block, CORE), core)

    corner = both_blocks(message[:share] * scale + added_part(core * share, panel_cols))
    state = jnp.concatenate([corner, jnp.eye(width, dtype=f32)], axis=1)

    calls = [(b, b + 1) for b in range(0, width // CHOL, 2)]
    state = eliminate_blocks(state, calls[0])
    two = (sums_32[share:] + after(other_two, state).astype(f32)).astype(bf16)
    got_two = send(two, FAR)
    state = eliminate_blocks(after(state, two), calls[1])
    sums_10 = mine_10 + after(other_10, state).astype(f32)
    one = sums_10[:share].astype(bf16)
    got_one = send(one, NEAR)
    state = eliminate_blocks(after(state, one), calls[2])
    state = eliminate_blocks(state, calls[3])
    start = position * share
    own = sums_10[share:] + got_one.astype(f32) + got_two.astype(f32)
    rest = own[:, : landmarks - width] * scale + added_part(start, other_cols)
    own_shift = lax.dynamic_slice_in_dim(shift, start, share, 1)
    rhs = (own[:, landmarks - width :] + highest(own_shift, target_sums)) / math.sqrt(
        ridge_weight * total_rows
    )
    added = both_blocks(added_part(core * share, other_cols))
    sums = both_blocks(after(part, state, added))
    panel, trailing = finish(scale, start, state, corner, sums, added, rest)
    return (rhs, panel, trailing)


def solution(mesh):
    local = local_16 if mesh.shape["dp"] == 16 else local_any
    in_specs = (P(("groups", "dp"), None), P(("groups", "dp"), None), P("groups"))
    out_specs = (P(("groups", "dp"), None), P(("groups", "dp"), None), P(("groups", "dp"), None))
    return jax.shard_map(local, mesh=mesh, in_specs=in_specs, out_specs=out_specs, check_vma=False)
```

```python
import functools
import math

import jax
import jax.numpy as jnp
from jax import lax
from jax.experimental import pallas as pl
from jax.experimental.pallas import tpu as pltpu
from jax.sharding import PartitionSpec as P

PB = 256


ridge_weight = 0.01


def sq_norms(row_block):
    wide_rows = row_block.astype(jnp.float32)
    return jnp.sum(wide_rows * wide_rows, axis=1)


def tanimoto(row_block, landmark_fps, landmark_norms):
    inner_prod = lax.dot_general(
        row_block, landmark_fps, (((1,), (1,)), ((), ())), preferred_element_type=jnp.float32
    )
    row_norms = sq_norms(row_block)
    return inner_prod / (row_norms[:, None] + landmark_norms[None, :] - inner_prod)


def local_any(fingerprints, targets, landmark_index):
    rows_dev = fingerprints.shape[0]
    devices = lax.axis_size("dp")
    total_rows = rows_dev * devices
    landmarks = landmark_index.shape[0]
    land_share = landmarks // devices
    position = lax.axis_index("dp")
    owner_dev = landmark_index // rows_dev
    offset = landmark_index % rows_dev
    is_mine = owner_dev == position
    capacity = 2 * land_share
    owner_onehot = (owner_dev[:, None] == jnp.arange(devices, dtype=jnp.int32)[None, :]).astype(
        jnp.int32
    )
    owner_rank = jnp.sum(jnp.cumsum(owner_onehot, axis=0) * owner_onehot, axis=1) - 1
    slot_rows = (
        jnp.zeros((capacity,), jnp.int32)
        .at[jnp.where(is_mine, owner_rank, capacity)]
        .set(offset, mode="drop")
    )
    packed = fingerprints[slot_rows]
    gathered = lax.all_gather(packed, "dp", axis=0, tiled=True)
    landmark_fps = gathered[owner_dev * capacity + owner_rank]
    landmark_norms = sq_norms(landmark_fps)
    kernel = tanimoto(fingerprints, landmark_fps, landmark_norms)
    col_total = lax.psum(jnp.sum(kernel, axis=0), "dp")
    col_mean = col_total / total_rows
    centred = (kernel - col_mean[None, :]).astype(jnp.bfloat16)
    joined = jnp.concatenate([centred, targets], axis=1)
    totals = lax.psum_scatter(
        lax.dot_general(
            centred, joined, (((0,), (0,)), ((), ())), preferred_element_type=jnp.float32
        ),
        "dp",
        scatter_dimension=0,
        tiled=True,
    )
    gram_rows = totals[:, :landmarks]
    rhs_rows = totals[:, landmarks:]
    rhs = rhs_rows / math.sqrt(ridge_weight * total_rows)
    own_fps = lax.dynamic_slice_in_dim(landmark_fps, position * land_share, land_share, 0)
    system_rows = gram_rows / (ridge_weight * total_rows) + tanimoto(
        own_fps, landmark_fps, landmark_norms
    )
    panel_width = PB
    column_block = lax.all_gather(system_rows[:, :panel_width], "dp", axis=0, tiled=True)
    corner = jnp.linalg.cholesky(column_block[:panel_width])
    panel_full = lax.linalg.triangular_solve(
        corner, column_block, left_side=False, lower=True, transpose_a=True
    )
    panel_own = lax.dynamic_slice_in_dim(panel_full, position * land_share, land_share, 0)
    trailing = system_rows - jnp.dot(panel_own, panel_full.T, precision=lax.Precision.HIGHEST)
    return (rhs, panel_own, trailing)


CORE = [(i, i ^ 1) for i in range(16)]
ROW = [(i, i ^ 2) for i in range(16)]
NEAR = [(i, i ^ 4) for i in range(16)]
FAR = [(i, i ^ 8) for i in range(16)]
LANES = 128
TILE = 256
MIB = 2**20
LITTLE = pl.CostEstimate(flops=1, transcendentals=0, bytes_accessed=1)


def send(x, perm):
    return lax.ppermute(x, "dp", perm)


def highest(a, b):
    return lax.dot_general(
        a,
        b,
        (((0,), (0,)), ((), ())),
        precision=lax.Precision.HIGHEST,
        preferred_element_type=jnp.float32,
    )


def dot_nt(a, b):
    return lax.dot_general(a, b, (((1,), (1,)), ((), ())), preferred_element_type=jnp.float32)


def dot_nn(a, b):
    return lax.dot_general(a, b, (((1,), (0,)), ((), ())), preferred_element_type=jnp.float32)


def after(x, *earlier):
    return lax.optimization_barrier((x,) + earlier)[0]


def vmem(count):
    return [pl.BlockSpec(memory_space=pltpu.VMEM)] * count


def spread(row_vector):
    return jnp.broadcast_to(row_vector, (LANES, LANES)).T


def stage_body(
    core_ref, land_ref, fps_ref, norms_ref, tgs_ref,
    ct_ref, rhs_ref, rest_ref, message_ref, lead_ref, column_ref,
    cent_ref, first_ref, left_ref, mean_ref,
):
    step = pl.program_id(0)
    rows = fps_ref.shape[0]
    base = pl.multiple_of(step * TILE, TILE)
    block = pl.multiple_of(core_ref[0] * LANES, LANES)
    tile = land_ref[...]
    wide = tile.astype(jnp.float32)
    land_norms = jnp.sum(wide * wide, axis=1, keepdims=True)
    total = jnp.zeros((TILE, 1), jnp.float32)
    for n in range(0, rows, TILE):
        inner = dot_nt(tile, fps_ref[n : n + TILE, :])
        kernel = inner / (norms_ref[:, n : n + TILE] + land_norms - inner)
        cent_ref[:, n : n + TILE] = kernel
        total = total + jnp.sum(kernel, axis=1, keepdims=True)
    mean = total * (1.0 / rows)
    for n in range(0, rows, TILE):
        cent = cent_ref[:, n : n + TILE] - mean
        cent_ref[:, n : n + TILE] = cent
        ct_ref[:, n : n + TILE] = cent.astype(jnp.bfloat16)
    own = cent_ref[pl.ds(block, LANES), :]
    low = (own - ct_ref[pl.ds(block, LANES), :].astype(jnp.float32)).astype(jnp.bfloat16)
    mean_ref[:, pl.ds(base, TILE)] = jnp.broadcast_to(mean, (TILE, LANES)).T[:1, :]

    @pl.when(step == 0)
    def _():
        left_ref[:LANES, :] = ct_ref[pl.ds(block, LANES), :]
        left_ref[LANES:, :] = tgs_ref[...]

    both = dot_nt(left_ref[...], ct_ref[...])
    first_ref[:, pl.ds(base, TILE)] = both[:LANES, :]
    cent_ref[:LANES, :TILE] = both[LANES:, :]
    high_part = cent_ref[:LANES, pl.ds(block, LANES)]
    rhs_ref[step] = (high_part + dot_nt(left_ref[LANES:, :], low)).T

    @pl.when(step == pl.num_programs(0) - 1)
    def _():
        lead = jnp.sum(first_ref[...], axis=0, keepdims=True)
        lead_ref[...] = lead
        lead_own = lead_ref[:, pl.ds(block, LANES)]
        mass = jnp.sum(lead_own, axis=1, keepdims=True)
        size = jnp.sum(jnp.abs(lead_own), axis=1, keepdims=True)
        usable = mass > 1e-3 * size
        weight = jnp.where(usable, 1.0 / jnp.where(usable, mass, 1.0), 0.0)
        mine = spread(lead_own) * weight
        for j in range(lead.shape[1] // LANES):
            cols = slice(j * LANES, (j + 1) * LANES)
            part = lead[:, cols]
            column_ref[cols, :] = spread(part) * weight
            rest = first_ref[:, cols] - mine * part
            if j < TILE // LANES:
                message_ref[:LANES, cols] = rest
            else:
                rest_ref[:, slice(cols.start - TILE, cols.stop - TILE)] = rest
        message_ref[LANES:, :] = jnp.zeros((message_ref.shape[0] - LANES, TILE), jnp.float32)
        for j in range(lead.shape[1] // TILE):
            cols = slice(j * TILE, (j + 1) * TILE)
            message_ref[LANES + j : LANES + j + 1, :] = mean_ref[:, cols]
            message_ref[LANES + 8 + j : LANES + 9 + j, :] = lead[:, cols]
        at = LANES + 16
        message_ref[at : at + 1, :LANES] = jnp.broadcast_to(weight, (1, LANES))
        sums = jnp.sum(tgs_ref[...].astype(jnp.float32), axis=1, keepdims=True)
        message_ref[at : at + 1, LANES:] = jnp.broadcast_to(sums, (LANES, LANES)).T[:1, :]


STATS = 24


def stage(core, landmark_fps, fps, norms, tgs):
    rows, length = fps.shape
    landmarks = landmark_fps.shape[0]
    steps = landmarks // TILE
    f32, bf16 = jnp.float32, jnp.bfloat16

    def whole(shape):
        return pl.BlockSpec(shape, lambda i, c: (0,) * len(shape))

    outs = [
        ((steps, LANES, LANES), f32),
        ((LANES, landmarks - TILE), f32),
        ((LANES + STATS, TILE), f32),
        ((1, landmarks), f32),
        ((landmarks, LANES), f32),
    ]
    return pl.pallas_call(
        stage_body,
        grid_spec=pltpu.PrefetchScalarGridSpec(
            num_scalar_prefetch=1,
            grid=(steps,),
            in_specs=[
                pl.BlockSpec((TILE, length), lambda i, c: (i, 0)),
                whole(fps.shape),
                whole(norms.shape),
                whole(tgs.shape),
            ],
            out_specs=[pl.BlockSpec((TILE, rows), lambda i, c: (i, 0))]
            + [whole(s) for s, _ in outs],
            scratch_shapes=[
                pltpu.VMEM((TILE, rows), f32),
                pltpu.VMEM((LANES, landmarks), f32),
                pltpu.VMEM((2 * LANES, rows), bf16),
                pltpu.VMEM((1, landmarks), f32),
            ],
        ),
        out_shape=[jax.ShapeDtypeStruct((landmarks, rows), bf16)]
        + [jax.ShapeDtypeStruct(s, d) for s, d in outs],
        compiler_params=pltpu.CompilerParams(vmem_limit_bytes=28 * MIB),
        name="stage",
    )(core, landmark_fps, fps, norms, tgs)


def pieces_body(at_ref, ct_ref, lead_ref, column_ref, rhs_ref, mine_ref, theirs_ref, left_ref):
    count = left_ref.shape[0] // LANES
    for p in range(count):
        at = pl.multiple_of(at_ref[p], LANES)
        left_ref[p * LANES : (p + 1) * LANES, :] = ct_ref[pl.ds(at, LANES), :]

    def store(p, cols, value):
        out = (mine_ref, theirs_ref)[p % 2]
        out[p // 2 * LANES : (p // 2 + 1) * LANES, cols] = value.astype(out.dtype)

    for t in range(1, ct_ref.shape[0] // TILE):
        for q in range(0, count, 2):
            got = dot_nt(
                left_ref[q * LANES : (q + 2) * LANES, :], ct_ref[t * TILE : (t + 1) * TILE, :]
            )
            for p in (q, q + 1):
                at = pl.multiple_of(at_ref[p], LANES)
                column = column_ref[pl.ds(at, LANES), :]
                for h in range(TILE // LANES):
                    lo = t * TILE + h * LANES
                    part = got[(p - q) * LANES : (p - q + 1) * LANES, h * LANES : (h + 1) * LANES]
                    part = part - column * lead_ref[:, lo : lo + LANES]
                    store(p, slice(lo - TILE, lo - TILE + LANES), part)
    for p in range(count):
        lo = ct_ref.shape[0] - TILE
        store(p, slice(lo, lo + LANES), rhs_ref[at_ref[p] // TILE])


def pieces(starts, ct, lead, column, rhs_part):
    shape = (len(starts) // 2 * LANES, ct.shape[0] - TILE + LANES)
    return pl.pallas_call(
        pieces_body,
        in_specs=[pl.BlockSpec(memory_space=pltpu.SMEM)] + vmem(4),
        out_specs=vmem(2),
        out_shape=[
            jax.ShapeDtypeStruct(shape, jnp.float32),
            jax.ShapeDtypeStruct(shape, jnp.bfloat16),
        ],
        scratch_shapes=[pltpu.VMEM((2 * shape[0], ct.shape[1]), jnp.bfloat16)],
        compiler_params=pltpu.CompilerParams(vmem_limit_bytes=28 * MIB),
        cost_estimate=LITTLE,
        name="pieces",
    )(jnp.stack(starts).astype(jnp.int32), ct, lead, column, rhs_part)


CHOL = 32


def exact_dot(a, b, dims=((1,), (0,))):
    return lax.dot_general(
        a, b, (dims, ((), ())), precision=lax.Precision.HIGHEST, preferred_element_type=jnp.float32
    )


def factor_body(blocks, state_ref, out_ref):
    size = state_ref.shape[0]
    out_ref[...] = state_ref[...]
    sub = lax.broadcasted_iota(jnp.int32, (CHOL, LANES), 0)
    lane = lax.broadcasted_iota(jnp.int32, (CHOL, LANES), 1)
    for b in blocks:
        lo, hi = b * CHOL, (b + 1) * CHOL
        diag = out_ref[lo:hi, lo:hi]
        work = jnp.concatenate(
            [
                diag,
                (sub == lane)[:, :CHOL].astype(jnp.float32),
                jnp.zeros((CHOL, LANES - 2 * CHOL), jnp.float32),
            ],
            axis=1,
        )

        for k in range(CHOL):
            col = jnp.broadcast_to(work[:, k : k + 1], work.shape)
            row = work[k : k + 1, :] / col[k : k + 1, :]
            work = work - jnp.where(sub > k, col, 0.0) * row
        pivots = jnp.sum(jnp.where(sub == lane, work, 0.0), axis=1, keepdims=True)
        inverse = work[:, CHOL : 2 * CHOL] / jnp.sqrt(pivots)
        done = exact_dot(inverse, out_ref[lo:hi, :])
        out_ref[lo:hi, :] = done
        if hi < size:
            left = hi // LANES * LANES
            cols = slice(left, size + -(-hi // LANES) * LANES)
            out_ref[hi:, cols] = out_ref[hi:, cols] - exact_dot(
                done[:, hi:size], done[:, cols], ((0,), (0,))
            )


def eliminate_blocks(state, blocks):
    return pl.pallas_call(
        functools.partial(factor_body, blocks),
        in_specs=vmem(1),
        out_specs=vmem(1)[0],
        out_shape=jax.ShapeDtypeStruct(state.shape, jnp.float32),
        compiler_params=pltpu.CompilerParams(vmem_limit_bytes=28 * MIB),
        cost_estimate=LITTLE,
        name="factor",
    )(state)


def finish_body(
    scale, at_ref, state_ref, corner_ref, sums_ref, added_ref, rest_ref,
    panel_ref, trailing_ref, factor_ref, own_ref,
):
    width = corner_ref.shape[0]
    start = pl.multiple_of(at_ref[0], LANES)
    inverse = state_ref[:, width:]
    own_ref[:, :width] = corner_ref[...]
    factor_ref[:, :width] = exact_dot(inverse, corner_ref[...])
    for lo in range(0, rest_ref.shape[1], TILE):
        cols = slice(lo, lo + TILE)
        rows = sums_ref[:, cols].astype(jnp.float32) * scale + added_ref[:, cols]
        own_ref[:, lo + width : lo + width + TILE] = rows
        factor_ref[:, lo + width : lo + width + TILE] = exact_dot(inverse, rows)
    panel = factor_ref[:, pl.ds(start, LANES)].T
    panel_ref[...] = panel
    first = own_ref[:, pl.ds(start, LANES)].T
    trailing_ref[:, :width] = first - exact_dot(panel, factor_ref[:, :width])
    for lo in range(0, rest_ref.shape[1], TILE):
        here = slice(lo + width, lo + width + TILE)
        trailing_ref[:, here] = rest_ref[:, lo : lo + TILE] - exact_dot(panel, factor_ref[:, here])


def finish(scale, start, state, corner, sums, added, rest):
    width, landmarks = corner.shape[0], rest.shape[1] + corner.shape[0]
    f32 = jnp.float32
    return pl.pallas_call(
        functools.partial(finish_body, scale),
        in_specs=[pl.BlockSpec(memory_space=pltpu.SMEM)] + vmem(5),
        out_specs=vmem(2),
        out_shape=[
            jax.ShapeDtypeStruct((LANES, width), f32),
            jax.ShapeDtypeStruct((LANES, landmarks), f32),
        ],
        scratch_shapes=[pltpu.VMEM((width, landmarks), f32), pltpu.VMEM((width, landmarks), f32)],
        compiler_params=pltpu.CompilerParams(vmem_limit_bytes=28 * MIB),
        name="finish",
    )(jnp.reshape(start, (1,)), state, corner, sums, added, rest)


def pack_body(at_ref, index_ref, fps_ref, packed_ref, slots_ref, key_ref, pick_ref):
    rows, landmarks = fps_ref.shape[0], index_ref.shape[1]
    capacity = packed_ref.shape[0]
    f32 = jnp.float32
    index = index_ref[...].astype(f32)
    owner = jnp.floor(index * (1.0 / rows))
    key_ref[1:2, :] = index - owner * rows
    device = lax.broadcasted_iota(jnp.int32, (16, TILE), 0).astype(f32)
    before = lax.broadcasted_iota(jnp.int32, (TILE, TILE), 0)
    before = (before < lax.broadcasted_iota(jnp.int32, (TILE, TILE), 1)).astype(jnp.bfloat16)
    owners = [owner[:, n : n + TILE] for n in range(0, landmarks, TILE)]
    owned = [(device == o).astype(f32) for o in owners]
    within = dot_nn(jnp.concatenate(owned, axis=0).astype(jnp.bfloat16), before)
    ahead = jnp.zeros((16, 1), f32)
    slot_in = lax.broadcasted_iota(jnp.int32, (capacity, TILE), 0).astype(f32)
    for b, o in enumerate(owners):
        counts = within[b * 16 : (b + 1) * 16, :] + ahead
        rank = jnp.sum(owned[b] * counts, axis=0, keepdims=True)
        ahead = ahead + jnp.sum(owned[b], axis=1, keepdims=True)
        slot = o * capacity + rank
        for h in range(0, TILE, LANES):
            lo = b * TILE + h
            slots_ref[lo : lo + LANES, :] = spread(slot[:, h : h + LANES])
        key = jnp.where(o == at_ref[0].astype(f32), rank, -1.0)
        pick_ref[:, b * TILE : (b + 1) * TILE] = (slot_in == key).astype(jnp.bfloat16)
    packed = jnp.zeros(packed_ref.shape, f32)
    for r in range(0, rows, TILE):
        row_in = lax.broadcasted_iota(jnp.int32, (TILE, landmarks), 0).astype(f32) + r
        here = (row_in == key_ref[1:2, :]).astype(jnp.bfloat16)
        chosen = dot_nt(pick_ref[...], here).astype(jnp.bfloat16)
        packed = packed + dot_nn(chosen, fps_ref[r : r + TILE, :])
    packed_ref[...] = packed.astype(jnp.bfloat16)


def pack(position, landmark_index, fingerprints):
    landmarks = landmark_index.shape[0]
    capacity = landmarks // 8
    return pl.pallas_call(
        pack_body,
        in_specs=[pl.BlockSpec(memory_space=pltpu.SMEM)] + vmem(2),
        out_specs=vmem(2),
        out_shape=[
            jax.ShapeDtypeStruct((capacity, fingerprints.shape[1]), jnp.bfloat16),
            jax.ShapeDtypeStruct((landmarks, LANES), jnp.float32),
        ],
        scratch_shapes=[
            pltpu.VMEM((8, landmarks), jnp.float32),
            pltpu.VMEM((capacity, landmarks), jnp.bfloat16),
        ],
        compiler_params=pltpu.CompilerParams(vmem_limit_bytes=28 * MIB),
        name="pack",
    )(jnp.reshape(position, (1,)), landmark_index[None, :], fingerprints)


def place_body(count, base_ref, slots_ref, *refs):
    chunks, before, out_ref = refs[:count], refs[count:-1], refs[-1]
    slots = slots_ref[...]
    lane = lax.broadcasted_iota(jnp.int32, slots.shape, 1).astype(jnp.float32)
    got = before[0][...].astype(jnp.float32) if before else jnp.zeros(out_ref.shape, jnp.float32)
    for n, chunk in enumerate(chunks):
        inside = slots - base_ref[n].astype(jnp.float32)
        chosen = jnp.concatenate(
            [
                (inside == lane + h).astype(jnp.float32)
                for h in range(0, chunk.shape[0], LANES)
            ],
            axis=1,
        )
        got = got + dot_nn(chosen.astype(jnp.bfloat16), chunk[...])
    out_ref[...] = got.astype(jnp.bfloat16)


def place(owners, chunks, slots, before=None):
    capacity, length = chunks[0].shape
    landmarks = slots.shape[0]
    tile = pl.BlockSpec((TILE, length), lambda i: (i, 0))
    extra = [] if before is None else [before]
    return pl.pallas_call(
        functools.partial(place_body, len(chunks)),
        grid=(landmarks // TILE,),
        in_specs=[
            pl.BlockSpec(memory_space=pltpu.SMEM),
            pl.BlockSpec((TILE, LANES), lambda i: (i, 0)),
        ]
        + [pl.BlockSpec((capacity, length), lambda i: (0, 0))] * len(chunks)
        + [tile] * len(extra),
        out_specs=tile,
        out_shape=jax.ShapeDtypeStruct((landmarks, length), jnp.bfloat16),
        compiler_params=pltpu.CompilerParams(vmem_limit_bytes=28 * MIB),
        name="place",
    )((jnp.stack(owners) * capacity).astype(jnp.int32), slots, *chunks, *extra)


def landmarks_everywhere(fingerprints, landmark_index):
    position = lax.axis_index("dp")
    packed, slots = pack(position, landmark_index, fingerprints)
    held = {0: packed}
    for perm, mask in ((FAR, 8), (NEAR, 4), (ROW, 2)):
        held[mask] = send(packed, perm)
    held[12] = send(held[8], NEAR)
    held[6] = send(held[4], ROW)
    held[10] = send(held[8], ROW)
    held[14] = send(held[12], ROW)
    result = None
    for masks in ((0, 2, 4, 8, 6, 12), (10, 14)):
        owners, chunks = [], []
        for m in masks:
            chunk = held[m]
            if m in (10, 14):
                chunk = after(chunk, result)
            owners += [position ^ m, position ^ m ^ 1]
            chunks += [chunk, send(chunk, CORE)]
        result = place(owners, chunks, slots, result)
    return result


def local_16(fingerprints, targets, landmark_index):
    rows_dev = fingerprints.shape[0]
    total_rows = rows_dev * 16
    landmarks = landmark_index.shape[0]
    share = landmarks // 16
    width = PB
    position = lax.axis_index("dp")
    core = position % 2
    row = (position // 2) % 2
    layer = position // 4
    scale = 1.0 / (ridge_weight * total_rows)

    fps = jnp.concatenate([fingerprints, send(fingerprints, CORE)], axis=0)
    tgs = jnp.concatenate([targets, send(targets, CORE)], axis=0)
    chip_rows = 2 * rows_dev
    landmark_fps = landmarks_everywhere(fingerprints, landmark_index)
    norms = sq_norms(landmark_fps)
    ct, rhs_part, rest_rows, message, lead, column = stage(
        jnp.reshape(core, (1,)), landmark_fps, fps, sq_norms(fps)[None, :], tgs.T
    )
    panel_cols, other_cols = slice(0, width), slice(width, landmarks)
    f32, bf16 = jnp.float32, jnp.bfloat16

    def gram_rows(masks, ct):
        starts = []
        for m in masks:
            there = ((layer ^ m) * 4 + core) * share
            starts += [there + row * 2 * share, there + (1 - row) * 2 * share]
        return pieces(starts, ct, lead, column, rhs_part)

    def merge(x, y):
        return jnp.concatenate([x[:share] + y[:share], x[share:], y[share:]], axis=0)

    planes = [[2 * j + c for j in range(8)] for c in range(2)]
    part = lax.psum(rest_rows, "dp", axis_index_groups=planes)
    message_row = send(message, ROW)
    mine_32, theirs_32 = gram_rows((3, 2), ct)
    other_32 = send(theirs_32, ROW)
    message = merge(message, after(message_row, mine_32))
    message_near = send(message, NEAR)
    mine_10, theirs_10 = gram_rows((1, 0), after(ct, message))
    other_10 = send(theirs_10, ROW)
    message = merge(message, after(message_near, mine_10))
    message_far = send(message, FAR)
    sums_32 = mine_32 + after(other_32, message).astype(f32)
    three = sums_32[:share].astype(bf16)
    other_two = send(three, NEAR)
    message = merge(message, after(message_far, three))

    stats = message[share:].reshape(8, STATS, TILE)
    means = stats[:, :8].reshape(8, landmarks)
    leads = stats[:, 8:16].reshape(8, landmarks)
    lead_weights, target_sums = stats[:, 16, :1], stats[:, 16, LANES:]
    shift = means - jnp.mean(means, axis=0, keepdims=True)
    left_terms = jnp.concatenate([shift * chip_rows, leads], axis=0)
    right_terms = jnp.concatenate([shift, leads * lead_weights], axis=0)

    def added_part(start, cols):
        rows_fps = lax.dynamic_slice_in_dim(landmark_fps, start, share, 0)
        terms = lax.dynamic_slice_in_dim(left_terms, start, share, 1)
        return highest(terms, right_terms[:, cols]) * scale + tanimoto(
            rows_fps, landmark_fps[cols], norms[cols]
        )

    def in_order(x, other, high):
        size = x.shape[0]
        return lax.dynamic_slice_in_dim(
            jnp.concatenate([x, other, x], axis=0), high * size, 2 * size, 0
        )

    def both_blocks(block):
        return in_order(block, send(block, CORE), core)

    corner = both_blocks(message[:share] * scale + added_part(core * share, panel_cols))
    state = jnp.concatenate([corner, jnp.eye(width, dtype=f32)], axis=1)

    calls = [(b, b + 1) for b in range(0, width // CHOL, 2)]
    state = eliminate_blocks(state, calls[0])
    two = (sums_32[share:] + after(other_two, state).astype(f32)).astype(bf16)
    got_two = send(two, FAR)
    state = eliminate_blocks(after(state, two), calls[1])
    sums_10 = mine_10 + after(other_10, state).astype(f32)
    one = sums_10[:share].astype(bf16)
    got_one = send(one, NEAR)
    state = eliminate_blocks(after(state, one), calls[2])
    state = eliminate_blocks(state, calls[3])
    start = position * share
    own = sums_10[share:] + got_one.astype(f32) + got_two.astype(f32)
    rest = own[:, : landmarks - width] * scale + added_part(start, other_cols)
    own_shift = lax.dynamic_slice_in_dim(shift, start, share, 1)
    rhs = (own[:, landmarks - width :] + highest(own_shift, target_sums)) / math.sqrt(
        ridge_weight * total_rows
    )
    added = both_blocks(added_part(core * share, other_cols))
    sums = both_blocks(after(part, state, added))
    panel, trailing = finish(scale, start, state, corner, sums, added, rest)
    return (rhs, panel, trailing)


def solution(mesh):
    local = local_16 if mesh.shape["dp"] == 16 else local_any
    in_specs = (P(("groups", "dp"), None), P(("groups", "dp"), None), P("groups"))
    out_specs = (P(("groups", "dp"), None), P(("groups", "dp"), None), P(("groups", "dp"), None))
    return jax.shard_map(local, mesh=mesh, in_specs=in_specs, out_specs=out_specs, check_vma=False)
```
